32 devices in a mesh: seq: 4 (over z), fsdp: 8 (over y, x, core).
Axes of the slice: x: 2, y: 2, z: 4, core: 2. Of those that a mesh axis runs over, the one named last changes fastest.
Arguments:
- tokens: bfloat16 [8, 512, 768], P('fsdp', 'seq'), may hold values from -6 to 6
- positions: int32 [8, 512], P('fsdp', 'seq'), may hold values from 0 to 5117, as said below
- norm1_gain: bfloat16 [768], P('fsdp'), may hold values from 0.5 to 1.5
- qkv_weight: bfloat16 [768, 2304], P('fsdp'), may hold values from -0.57735027 to 0.57735027, as said below
- out_weight: bfloat16 [768, 768], P('fsdp'), may hold values from -6 to 6
- norm2_gain: bfloat16 [768], P('fsdp'), may hold values from 0.5 to 1.5
- in_weight: bfloat16 [768, 2304], P('fsdp'), may hold values from -0.21875 to 0.21875
- down_weight: bfloat16 [1152, 768], P(None, 'fsdp'), may hold values from -0.1875 to 0.1875
- cotangent: bfloat16 [8, 512, 768], P('fsdp', 'seq'), may hold values from -6 to 6
Outputs:
- block_out: bfloat16 [8, 512, 768], P('fsdp', 'seq')
- input_grad: bfloat16 [8, 512, 768], P('fsdp', 'seq')
- qkv_weight_grad: float32 [768, 2304], P('fsdp')
- out_weight_grad: float32 [768, 768], P('fsdp')
- in_weight_grad: float32 [768, 2304], P('fsdp')
- down_weight_grad: float32 [1152, 768], P(None, 'fsdp')
- norm1_gain_grad: float32 [768], P('fsdp')
- norm2_gain_grad: float32 [768], P('fsdp')
The draws below stay inside these ranges and needn't reach their ends.
Inputs may be any that keep to these rules, and one draw needn't show every extreme that they name: Along each sequence the positions rise by 1 or 2 from one token to the next. `qkv_weight`: A projection matrix; every entry lies within 16 / sqrt(768) of zero.
All inputs are finite; a program needn't handle non-finite values.
Results may differ from the reference program's by a relative error of at most 0.019.
Values may be sent and summed in bfloat16 or wider, within the bound.
A program may use at most 128 MiB of HBM per device.

```python
import jax
import jax.numpy as jnp
from jax import lax

D = 768
HEADS = 12
HEAD_DIM = 64
FF = 1152
LEN = 512
SEQS = 8


def draw_positions(key, part):
    offsets = jax.random.randint(jax.random.fold_in(key, 11), (SEQS, 1), 0, 4096)
    strides = jax.random.randint(jax.random.fold_in(key, 12), (SEQS, LEN), 1, 3)
    row_index = jnp.arange(SEQS, dtype=jnp.int32)[:, None]
    offsets = jnp.where(row_index == 0, 0, offsets)
    offsets = jnp.where(row_index == SEQS - 1, 4095, offsets)
    strides = jnp.where(row_index == SEQS - 1, 2, strides)
    rising = jnp.cumsum(strides, axis=1) - strides[:, :1]
    return (offsets + rising).astype(jnp.int32)


def draw_qkv_weight(key, part):
    base = jnp.clip(jax.random.normal(jax.random.fold_in(key, 21), (D, 3 * D), jnp.float32), -4.0, 4.0) * D ** (-0.5)
    return base.astype(jnp.bfloat16)


def block_scale(key, dims, pieces, smallest, largest):
    loudness = 1.0
    for dim, shards_of in pieces:
        heights = jax.random.uniform(jax.random.fold_in(jax.random.fold_in(key, 6), dim), (shards_of,), jnp.float32, smallest / len(pieces), largest / len(pieces))
        loudness = loudness * jnp.repeat(jnp.exp(heights), dims[dim] // shards_of).reshape((-1,) + (1,) * (len(dims) - 1 - dim))
    return loudness


def gaussian(own_key, dims, deviation, reach, split=(), kind=jnp.bfloat16):
    gain = block_scale(own_key, dims, split, -0.22, 0.18) if split else 1.0
    entries = jax.random.normal(own_key, dims, jnp.float32) * deviation * gain
    return jnp.minimum(jnp.maximum(entries, -reach), reach).astype(kind)


def setup_inputs(seed: int = 0) -> dict:
    splits = jax.random.split(jax.random.key(seed), 10)
    return {
        "tokens": gaussian(splits[0], (SEQS, LEN, D), 1.0, 6.0, ((0, 8), (1, 4))),
        "positions": draw_positions(jax.random.fold_in(splits[9], 71), 0),
        "norm1_gain": jnp.clip(1.0 + 0.1 * jax.random.normal(splits[2], (D,), jnp.float32), 0.5, 1.5).astype(jnp.bfloat16),
        "qkv_weight": draw_qkv_weight(jax.random.fold_in(splits[9], 71), 0),
        "out_weight": gaussian(splits[4], (D, D), (0.036 * LEN ** 0.5), 6.0, ((0, 8),)),
        "norm2_gain": jnp.clip(1.0 + 0.1 * jax.random.normal(splits[5], (D,), jnp.float32), 0.5, 1.5).astype(jnp.bfloat16),
        "in_weight": gaussian(splits[6], (D, 2 * FF), D ** -0.5, 0.21875, ((0, 8),)),
        "down_weight": gaussian(splits[7], (FF, D), FF ** -0.5, 0.1875, ((1, 8),)),
        "cotangent": gaussian(splits[8], (SEQS, LEN, D), 1.0, 6.0, ((0, 8), (1, 4))),
    }


eps = 1e-05
theta = 160000.0

def layer_norm(values, gain_vec):
    middle = lax.optimization_barrier(jnp.mean(values, axis=-1, keepdims=True))
    centred = values - middle
    inverse = lax.rsqrt(lax.optimization_barrier(jnp.mean(centred * centred, axis=-1, keepdims=True)) + eps)
    scaled = centred * inverse
    return (scaled * gain_vec, scaled, inverse)

def norm_back(upstream, scaled, inverse, gain_vec):
    gain_grad = lax.optimization_barrier(jnp.sum(upstream * scaled, axis=0))
    weighted = upstream * gain_vec
    result = inverse * (weighted - lax.optimization_barrier(jnp.mean(weighted, axis=-1, keepdims=True)) - scaled * lax.optimization_barrier(jnp.mean(weighted * scaled, axis=-1, keepdims=True)))
    return (result, gain_grad)

def rotary_tables(positions, head_size):
    half_dim = head_size // 2
    frequency = theta ** (-jnp.arange(half_dim, dtype=jnp.float32) / half_dim)
    angles = positions.astype(jnp.float32)[..., None] * frequency
    return (jnp.cos(angles)[..., None, :], jnp.sin(angles)[..., None, :])

def rotate(values, cosine_table, sine_table):
    half_dim = values.shape[-1] // 2
    first_half = values[..., :half_dim]
    second_half = values[..., half_dim:]
    return jnp.concatenate([first_half * cosine_table - second_half * sine_table, second_half * cosine_table + first_half * sine_table], axis=-1)

def rotate_back(values, cosine_table, sine_table):
    half_dim = values.shape[-1] // 2
    first_half = values[..., :half_dim]
    second_half = values[..., half_dim:]
    return jnp.concatenate([first_half * cosine_table + second_half * sine_table, second_half * cosine_table - first_half * sine_table], axis=-1)

def gelu_slope(values):
    return 0.5 * (1.0 + lax.erf(values * 0.7071067811865476)) + values * jnp.exp(-0.5 * values * values) * 0.3989422804014327

def sequence_pass(weight_set, tokens, positions, cotangent):
    qkv_weight, out_weight, in_weight, down_weight, gain_one, gain_two = weight_set
    score_scale = HEAD_DIM ** (-0.5)
    f32 = jnp.float32
    low = jnp.bfloat16
    inputs = tokens.astype(f32)
    normed_one, scaled_one, inverse_one = layer_norm(inputs, gain_one)
    normed_one = normed_one.astype(low)
    projected = jnp.dot(normed_one, qkv_weight, preferred_element_type=f32).reshape(LEN, 3, HEADS, HEAD_DIM)
    cosine_table, sine_table = rotary_tables(positions, HEAD_DIM)
    queries = rotate(projected[:, 0], cosine_table, sine_table).astype(low)
    key_rows = rotate(projected[:, 1], cosine_table, sine_table).astype(low)
    value_rows = projected[:, 2].astype(low)
    scores = jnp.einsum('qhd,khd->hqk', queries.astype(f32), key_rows.astype(f32)) * score_scale
    totals = jax.nn.logsumexp(scores, axis=-1)
    probs = jnp.exp(scores - totals[..., None])
    probs_low = probs.astype(low)
    attended = jnp.einsum('hqk,khd->qhd', probs_low.astype(f32), value_rows.astype(f32)).astype(low)
    attended_flat = attended.reshape(LEN, D)
    residual = inputs + jnp.dot(attended_flat, out_weight, preferred_element_type=f32)
    normed_two, scaled_two, inverse_two = layer_norm(residual, gain_two)
    normed_two = normed_two.astype(low)
    lifted = jnp.dot(normed_two, in_weight, preferred_element_type=f32)
    act_input = lifted[:, :FF]
    gate_part = lifted[:, FF:]
    activated = jax.nn.gelu(act_input, approximate=False)
    gated = (activated * gate_part).astype(low)
    block_out = (residual + jnp.dot(gated, down_weight, preferred_element_type=f32)).astype(low)
    down_grad = jnp.dot(gated.T, cotangent, preferred_element_type=f32)
    gated_grad = jnp.dot(cotangent, down_weight.T, preferred_element_type=f32)
    lifted_grad = jnp.concatenate([gated_grad * gate_part * gelu_slope(act_input), gated_grad * activated], axis=1).astype(low)
    in_grad = jnp.dot(normed_two.T, lifted_grad, preferred_element_type=f32)
    normed_two_grad = jnp.dot(lifted_grad, in_weight.T, preferred_element_type=f32)
    residual_part, gain_two_grad = norm_back(normed_two_grad, scaled_two, inverse_two, gain_two)
    residual_grad = cotangent.astype(f32) + residual_part
    residual_low = residual_grad.astype(low)
    out_grad = jnp.dot(attended_flat.T, residual_low, preferred_element_type=f32)
    attended_grad = jnp.dot(residual_low, out_weight.T, preferred_element_type=f32).astype(low).reshape(LEN, HEADS, HEAD_DIM)
    grad_f = attended_grad.astype(f32)
    delta_rows = lax.optimization_barrier(jnp.sum(grad_f * attended.astype(f32), axis=-1)).T
    value_grad = jnp.einsum('hqk,qhd->khd', probs_low.astype(f32), grad_f).astype(low)
    prob_grad = jnp.einsum('qhd,khd->hqk', grad_f, value_rows.astype(f32))
    score_grad = (probs * (prob_grad - delta_rows[..., None])).astype(low).astype(f32)
    query_grad = (jnp.einsum('hqk,khd->qhd', score_grad, key_rows.astype(f32)) * score_scale).astype(low)
    key_grad = (jnp.einsum('hqk,qhd->khd', score_grad, queries.astype(f32)) * score_scale).astype(low)
    qkv_grad = jnp.stack([rotate_back(query_grad.astype(f32), cosine_table, sine_table), rotate_back(key_grad.astype(f32), cosine_table, sine_table), value_grad.astype(f32)], axis=1).reshape(LEN, 3 * D).astype(low)
    qkv_grad_w = jnp.dot(normed_one.T, qkv_grad, preferred_element_type=f32)
    normed_one_grad = jnp.dot(qkv_grad, qkv_weight.T, preferred_element_type=f32)
    input_part, gain_one_grad = norm_back(normed_one_grad, scaled_one, inverse_one, gain_one)
    input_grad = (residual_grad + input_part).astype(low)
    return ((block_out, input_grad), (qkv_grad_w, out_grad, in_grad, down_grad, gain_one_grad, gain_two_grad))

def reference(tokens, positions, norm1_gain, qkv_weight, out_weight, norm2_gain, in_weight, down_weight, cotangent):
    weight_set = (qkv_weight, out_weight, in_weight, down_weight, norm1_gain.astype(jnp.float32), norm2_gain.astype(jnp.float32))

    def advance(carry, inputs):
        outputs, grads = sequence_pass(weight_set, inputs[0], inputs[1], inputs[2])
        return (jax.tree.map(lambda left, right: left + right, carry, grads), outputs)
    start = (jnp.zeros((D, 3 * D), jnp.float32), jnp.zeros((D, D), jnp.float32), jnp.zeros((D, 2 * FF), jnp.float32), jnp.zeros((FF, D), jnp.float32), jnp.zeros((D,), jnp.float32), jnp.zeros((D,), jnp.float32))
    grads, outputs = lax.scan(advance, start, (tokens, positions, cotangent))
    return (outputs[0], outputs[1], grads[0], grads[1], grads[2], grads[3], grads[4], grads[5])
```

```python
import functools

import jax
import jax.numpy as jnp
from jax import lax
from jax.experimental import pallas as pl
from jax.experimental.pallas import tpu as pltpu
from jax.sharding import PartitionSpec as P

HEADS = 12
HEAD_DIM = 64
MESH = pl.DeviceIdType.MESH

eps = 1e-05
theta = 160000.0


def exchange_kernel(kinds, seq_n, fsdp_n, *refs):
    count = len(kinds)
    ins = refs[:count]
    outs = refs[count : 2 * count]
    rest = list(refs[2 * count :])
    z = lax.axis_index("seq")
    f = lax.axis_index("fsdp")
    pairs = fsdp_n // 2
    chip = f // 2
    core = f % 2
    partner = chip * 2 + 1 - core
    on_seq = any(kind in ("gather", "swap") for kind in kinds)
    on_fsdp = any(kind in ("spread", "reduce") for kind in kinds)

    barrier = pltpu.get_barrier_semaphore()
    waits = 0
    if on_seq:
        for d in range(1, seq_n):
            pl.semaphore_signal(
                barrier, inc=1, device_id={"seq": (z + d) % seq_n}, device_id_type=MESH
            )
        waits += seq_n - 1
    if on_fsdp:
        for d in range(1, pairs):
            pl.semaphore_signal(
                barrier,
                inc=1,
                device_id={"fsdp": ((chip + d) % pairs) * 2 + core},
                device_id_type=MESH,
            )
        pl.semaphore_signal(barrier, inc=1, device_id={"fsdp": partner}, device_id_type=MESH)
        waits += pairs
    pl.semaphore_wait(barrier, waits)

    def remote(src, dst, send, recv, where):
        return pltpu.make_async_remote_copy(
            src_ref=src,
            dst_ref=dst,
            send_sem=send,
            recv_sem=recv,
            device_id=where,
            device_id_type=MESH,
        )

    work = []
    for kind, src, dst in zip(kinds, ins, outs):
        extra = [rest.pop(0) for _ in range({"gather": 3, "swap": 3, "spread": 5, "reduce": 6}[kind])]
        work.append((kind, src, dst, extra))
    finish = []

    for kind, src, dst, extra in work:
        if kind == "reduce":
            held, total, send_a, recv_a, send_b, recv_b = extra
            for d in range(pairs):
                block = ((chip + d) % pairs) * 2
                remote(
                    src.at[block + 1 - core], held.at[d], send_a.at[d], recv_a.at[d], {"fsdp": partner}
                ).start()
    for kind, src, dst, extra in work:
        if kind in ("gather", "swap"):
            send, recv, own = extra
            for d in range(1, seq_n):
                to = (z + d) % seq_n
                piece = src if kind == "gather" else src.at[to]
                copy = remote(piece, dst.at[z], send.at[d], recv.at[d], {"seq": to})
                copy.start()
                finish.append(copy.wait_send)
                origin = (z + seq_n - d) % seq_n
                arrival = remote(piece, dst.at[origin], send.at[d], recv.at[d], {"seq": to})
                finish.append(arrival.wait_recv)
            local_copy = pltpu.make_async_copy(
                src if kind == "gather" else src.at[z], dst.at[z], own.at[0]
            )
            local_copy.start()
            finish.append(local_copy.wait)
        elif kind == "spread":
            send_a, recv_a, send_b, recv_b, own = extra
            for d in range(1, pairs):
                copy = remote(
                    src,
                    dst.at[f],
                    send_a.at[d],
                    recv_a.at[d],
                    {"fsdp": ((chip + d) % pairs) * 2 + core},
                )
                copy.start()
                finish.append(copy.wait_send)
            copy = remote(src, dst.at[f], send_b.at[0], recv_b.at[0], {"fsdp": partner})
            copy.start()
            finish.append(copy.wait_send)
            local_copy = pltpu.make_async_copy(src, dst.at[f], own.at[0])
            local_copy.start()
            finish.append(local_copy.wait)
    for kind, src, dst, extra in work:
        if kind == "reduce":
            held, total, send_a, recv_a, send_b, recv_b = extra
            for d in list(range(1, pairs)) + [0]:
                block = ((chip + d) % pairs) * 2
                pair_copy = remote(
                    src.at[block + 1 - core], held.at[d], send_a.at[d], recv_a.at[d], {"fsdp": partner}
                )
                pair_copy.wait_recv()
                finish.append(pair_copy.wait_send)
                value = (
                    src[block + core].astype(jnp.float32) + held[d].astype(jnp.float32)
                ).astype(src.dtype)
                if d == 0:
                    dst[0] = value
                else:
                    total[d] = value
                    copy = remote(
                        total.at[d], dst.at[d], send_b.at[d], recv_b.at[d], {"fsdp": block + core}
                    )
                    copy.start()
                    finish.append(copy.wait)
    for d in range(1, pairs):
        for kind, src, dst, extra in work:
            if kind == "spread":
                send_a, recv_a, send_b, recv_b, own = extra
                origin = ((chip + pairs - d) % pairs) * 2 + core
                remote(src, dst.at[origin], send_a.at[d], recv_a.at[d], {"fsdp": partner}).wait_recv()
                copy = remote(
                    dst.at[origin], dst.at[origin], send_b.at[d], recv_b.at[d], {"fsdp": partner}
                )
                copy.start()
                finish.append(copy.wait_send)
    for kind, src, dst, extra in work:
        if kind == "spread":
            send_a, recv_a, send_b, recv_b, own = extra
            for d in range(pairs):
                origin = ((chip + pairs - d) % pairs) * 2 + 1 - core
                finish.append(
                    remote(
                        src, dst.at[origin], send_b.at[d], recv_b.at[d], {"fsdp": partner}
                    ).wait_recv
                )
    for wait in finish:
        wait()


def exchange(kinds, arrays, collective_id):
    seq_n = lax.axis_size("seq")
    fsdp_n = lax.axis_size("fsdp")
    pairs = fsdp_n // 2
    shapes = []
    scratch = []
    dma = pltpu.SemaphoreType.DMA
    for kind, array in zip(kinds, arrays):
        if kind == "gather":
            shapes.append((seq_n,) + array.shape)
            scratch += [dma((seq_n,)), dma((seq_n,)), dma((1,))]
        elif kind == "swap":
            shapes.append(array.shape)
            scratch += [dma((seq_n,)), dma((seq_n,)), dma((1,))]
        elif kind == "spread":
            shapes.append((fsdp_n,) + array.shape)
            scratch += [dma((pairs,))] * 4 + [dma((1,))]
        else:
            shapes.append((pairs,) + array.shape[1:])
            scratch += [pltpu.VMEM((pairs,) + array.shape[1:], array.dtype)] * 2
            scratch += [dma((pairs,))] * 4
    space = pl.BlockSpec(memory_space=pltpu.VMEM)
    return pl.pallas_call(
        functools.partial(exchange_kernel, tuple(kinds), seq_n, fsdp_n),
        out_shape=[jax.ShapeDtypeStruct(s, a.dtype) for s, a in zip(shapes, arrays)],
        in_specs=[space] * len(kinds),
        out_specs=[space] * len(kinds),
        scratch_shapes=scratch,
        compiler_params=pltpu.CompilerParams(collective_id=collective_id, has_side_effects=True),
        name=f"exchange_{collective_id}",
    )(*arrays)


def layer_norm(values, gain_vec):
    middle = jnp.mean(values, axis=-1, keepdims=True)
    centred = values - middle
    inverse = lax.rsqrt(jnp.mean(centred * centred, axis=-1, keepdims=True) + eps)
    scaled = centred * inverse
    return (scaled * gain_vec, scaled, inverse)


def norm_back(upstream, scaled, inverse, gain_vec):
    weighted = upstream * gain_vec
    return inverse * (
        weighted
        - jnp.mean(weighted, axis=-1, keepdims=True)
        - scaled * jnp.mean(weighted * scaled, axis=-1, keepdims=True)
    )


def rotary_tables(positions, head_size):
    half_dim = head_size // 2
    frequency = theta ** (-jnp.arange(half_dim, dtype=jnp.float32) / half_dim)
    angles = positions.astype(jnp.float32)[..., None] * frequency
    return (jnp.cos(angles), jnp.sin(angles))


def rotate(values, cosine_table, sine_table):
    half_dim = values.shape[-1] // 2
    first_half = values[..., :half_dim]
    second_half = values[..., half_dim:]
    return jnp.concatenate(
        [
            first_half * cosine_table - second_half * sine_table,
            second_half * cosine_table + first_half * sine_table,
        ],
        axis=-1,
    )


def gelu_slope(values):
    return (
        0.5 * (1.0 + lax.erf(values * 0.7071067811865476))
        + values * jnp.exp(-0.5 * values * values) * 0.3989422804014327
    )


def dot(left, right, left_dim=1, right_dim=0):
    return lax.dot_general(
        left, right, (((left_dim,), (right_dim,)), ((), ())), preferred_element_type=jnp.float32
    )


def local(
    tokens,
    positions,
    norm1_gain,
    qkv_weight,
    out_weight,
    norm2_gain,
    in_weight,
    down_weight,
    cotangent,
):
    f32 = jnp.float32
    low = jnp.bfloat16
    groups = lax.axis_size("seq")
    fsdp_n = lax.axis_size("fsdp")
    z = lax.axis_index("seq")
    seq_dev, span_len, width = tokens.shape
    rows = seq_dev * span_len
    length = span_len * groups
    local_heads = HEADS // groups
    group_width = local_heads * HEAD_DIM
    shard = qkv_weight.shape[0]
    ff = down_weight.shape[0]
    ff_part = ff // groups
    scale = HEAD_DIM ** (-0.5)

    qkv_part = lax.dynamic_index_in_dim(
        qkv_weight.reshape(shard, 3, groups, group_width), z, 2, keepdims=False
    ).reshape(shard, 3 * group_width)
    in_part = lax.dynamic_index_in_dim(
        in_weight.reshape(shard, 2, groups, ff_part), z, 2, keepdims=False
    ).reshape(shard, 2 * ff_part)
    down_part = lax.dynamic_slice_in_dim(down_weight, z * ff_part, ff_part, 0).T
    gains = jnp.stack([norm1_gain, norm2_gain])
    own_tokens = tokens.reshape(rows, width)
    own_cotangent = cotangent.reshape(rows, width)

    def whole(stack):
        w = stack.shape[-1]
        return jnp.swapaxes(stack.reshape(groups, seq_dev, span_len, w), 0, 1).reshape(
            seq_dev * length, w
        )

    def spans(full):
        w = full.shape[-1]
        return jnp.swapaxes(full.reshape(seq_dev, groups, span_len, w), 0, 1).reshape(
            groups, rows, w
        )

    all_tokens, all_cot, all_pos, w_qkv, w_out, w_in, w_down, all_gains = exchange(
        ["gather", "gather", "gather", "spread", "spread", "spread", "spread", "spread"],
        [own_tokens, own_cotangent, positions, qkv_part, out_weight, in_part, down_part, gains],
        0,
    )
    all_tokens = whole(all_tokens)
    all_cot = whole(all_cot)
    all_pos = jnp.swapaxes(all_pos, 0, 1).reshape(seq_dev, length)
    w_qkv = w_qkv.reshape(width, 3 * group_width)
    w_out = w_out.reshape(width, width)
    w_in = w_in.reshape(width, 2 * ff_part)
    w_down = w_down.reshape(width, ff_part)
    gain_one = all_gains[:, 0].reshape(width).astype(f32)
    gain_two = all_gains[:, 1].reshape(width).astype(f32)

    normed_one, scaled_full, _ = layer_norm(all_tokens.astype(f32), gain_one)
    normed_one = normed_one.astype(low)
    projected = dot(normed_one, w_qkv).reshape(seq_dev, length, 3, local_heads, HEAD_DIM)
    projected = projected.transpose(2, 0, 3, 1, 4)
    cosine, sine = rotary_tables(all_pos, HEAD_DIM)
    cosine = cosine[:, None]
    sine = sine[:, None]
    query = rotate(projected[0], cosine, sine).astype(low)
    key = rotate(projected[1], cosine, sine).astype(low)
    value = projected[2].astype(low)
    scores = jnp.einsum("bhqd,bhkd->bhqk", query, key, preferred_element_type=f32) * scale
    totals = jax.nn.logsumexp(scores, axis=-1, keepdims=True)
    probs = jnp.exp(scores - totals)
    probs_low = probs.astype(low)
    attended = jnp.einsum("bhqk,bhkd->bhqd", probs_low, value, preferred_element_type=f32).astype(
        low
    )

    def to_rows(heads):
        return heads.transpose(0, 2, 1, 3).reshape(seq_dev * length, group_width)

    (mixed,) = exchange(["swap"], [spans(to_rows(attended))], 1)
    mixed = jnp.swapaxes(mixed, 0, 1).reshape(rows, width)
    inputs = own_tokens.astype(f32)
    residual = inputs + dot(mixed, w_out)
    normed_two, scaled_two, inverse_two = layer_norm(residual, gain_two)
    normed_two = normed_two.astype(low)
    (normed_full,) = exchange(["gather"], [normed_two], 2)
    normed_full = whole(normed_full)
    lifted = dot(normed_full, w_in)
    act = lifted[:, :ff_part]
    gate = lifted[:, ff_part:]
    activated = jax.nn.gelu(act, approximate=False)
    gated = (activated * gate).astype(low)
    gated_grad = dot(all_cot, w_down)
    lifted_grad = jnp.concatenate(
        [gated_grad * gate * gelu_slope(act), gated_grad * activated], axis=1
    ).astype(low)
    ffn_part = dot(gated, w_down, 1, 1).astype(low)
    normed_grad_part = dot(lifted_grad, w_in, 1, 1).astype(low)
    ffn_parts, normed_grad_parts = exchange(
        ["swap", "swap"], [spans(ffn_part), spans(normed_grad_part)], 3
    )
    block_out = (residual + jnp.sum(ffn_parts.astype(f32), axis=0)).astype(low)
    normed_two_grad = jnp.sum(normed_grad_parts.astype(f32), axis=0)
    gain_two_grad = jnp.sum(normed_two_grad * scaled_two, axis=0)
    residual_grad = own_cotangent.astype(f32) + norm_back(
        normed_two_grad, scaled_two, inverse_two, gain_two
    )
    residual_low = residual_grad.astype(low)
    mixed_grad = dot(residual_low, w_out, 1, 1).astype(low)
    (head_grad,) = exchange(
        ["swap"], [jnp.swapaxes(mixed_grad.reshape(rows, groups, group_width), 0, 1)], 4
    )
    head_grad = whole(head_grad).reshape(seq_dev, length, local_heads, HEAD_DIM)
    head_grad = head_grad.transpose(0, 2, 1, 3)
    delta = jnp.sum(head_grad.astype(f32) * attended.astype(f32), axis=-1, keepdims=True)
    value_grad = jnp.einsum("bhqk,bhqd->bhkd", probs_low, head_grad, preferred_element_type=f32)
    prob_grad = jnp.einsum("bhqd,bhkd->bhqk", head_grad, value, preferred_element_type=f32)
    score_grad = (probs * (prob_grad - delta)).astype(low)
    query_grad = jnp.einsum("bhqk,bhkd->bhqd", score_grad, key, preferred_element_type=f32) * scale
    key_grad = jnp.einsum("bhqk,bhqd->bhkd", score_grad, query, preferred_element_type=f32) * scale
    qkv_grad = jnp.concatenate(
        [
            to_rows(rotate(query_grad.astype(low).astype(f32), cosine, -sine).astype(low)),
            to_rows(rotate(key_grad.astype(low).astype(f32), cosine, -sine).astype(low)),
            to_rows(value_grad.astype(low)),
        ],
        axis=1,
    )
    normed_one_grad_part = dot(qkv_grad, w_qkv, 1, 1)
    gain_one_grad = jnp.sum(normed_one_grad_part * scaled_full, axis=0)

    qkv_term = dot(normed_one, qkv_grad, 0, 0).astype(low)
    in_term = dot(normed_full, lifted_grad, 0, 0).astype(low)
    down_term = dot(all_cot, gated, 0, 0).astype(low)
    out_term = dot(mixed, residual_low, 0, 0).astype(low)
    gain_terms = jnp.stack(
        [gain_one_grad.reshape(fsdp_n, shard), gain_two_grad.reshape(fsdp_n, shard)], axis=1
    )
    parts = exchange(
        ["swap", "reduce", "reduce", "reduce", "reduce", "reduce"],
        [spans(normed_one_grad_part.astype(low))]
        + [t.reshape(fsdp_n, shard, t.shape[1]) for t in (qkv_term, in_term, down_term, out_term)]
        + [gain_terms],
        5,
    )
    normed_one_grad = jnp.sum(parts[0].astype(f32), axis=0)
    _, scaled_one, inverse_one = layer_norm(inputs, gain_one)
    input_grad = (
        residual_grad + norm_back(normed_one_grad, scaled_one, inverse_one, gain_one)
    ).astype(low)
    owned = [jnp.sum(p.astype(f32), axis=0).astype(p.dtype) for p in parts[1:]]
    qkv_all, in_all, down_all, out_all, gain_all = exchange(["gather"] * 5, owned, 6)
    qkv_out = (
        qkv_all.reshape(groups, shard, 3, group_width)
        .transpose(1, 2, 0, 3)
        .reshape(shard, 3 * width)
        .astype(f32)
    )
    in_out = (
        in_all.reshape(groups, shard, 2, ff_part)
        .transpose(1, 2, 0, 3)
        .reshape(shard, 2 * ff)
        .astype(f32)
    )
    down_out = down_all.transpose(0, 2, 1).reshape(ff, shard).astype(f32)
    out_out = jnp.sum(out_all.astype(f32), axis=0)
    gain_out = jnp.sum(gain_all, axis=0)
    return (
        block_out.reshape(seq_dev, span_len, width),
        input_grad.reshape(seq_dev, span_len, width),
        qkv_out,
        out_out,
        in_out,
        down_out,
        gain_out[0],
        gain_out[1],
    )


def solution(mesh):
    in_specs = (
        P("fsdp", "seq", None),
        P("fsdp", "seq"),
        P("fsdp"),
        P("fsdp", None),
        P("fsdp", None),
        P("fsdp"),
        P("fsdp", None),
        P(None, "fsdp"),
        P("fsdp", "seq", None),
    )
    out_specs = (
        P("fsdp", "seq", None),
        P("fsdp", "seq", None),
        P("fsdp", None),
        P("fsdp", None),
        P("fsdp", None),
        P(None, "fsdp"),
        P("fsdp"),
        P("fsdp"),
    )
    return jax.shard_map(local, mesh=mesh, in_specs=in_specs, out_specs=out_specs, check_vma=False)
```

```python
import functools

import jax
import jax.numpy as jnp
from jax import lax
from jax.experimental import pallas as pl
from jax.experimental.pallas import tpu as pltpu
from jax.sharding import PartitionSpec as P

HEADS = 12
HEAD_DIM = 64
MESH = pl.DeviceIdType.MESH

eps = 1e-05
theta = 160000.0


EXTRA = {"gather": 4, "swap": 3, "spread": 5, "fold": 8, "grad": 11}


def exchange_kernel(kinds, seq_n, fsdp_n, *refs):
    f32 = jnp.float32
    count = len(kinds)
    ins = refs[:count]
    outs = refs[count : 2 * count]
    rest = list(refs[2 * count :])
    z = lax.axis_index("seq")
    f = lax.axis_index("fsdp")
    pairs = fsdp_n // 2
    chip = f // 2
    core = f % 2
    partner = chip * 2 + 1 - core
    on_seq = any(kind != "spread" for kind in kinds)
    on_fsdp = any(kind in ("spread", "grad") for kind in kinds)

    barrier = pltpu.get_barrier_semaphore()
    waits = 0
    if on_seq:
        for d in range(1, seq_n):
            pl.semaphore_signal(
                barrier, inc=1, device_id={"seq": (z + d) % seq_n}, device_id_type=MESH
            )
        waits += seq_n - 1
    if on_fsdp:
        for d in range(1, pairs):
            pl.semaphore_signal(
                barrier,
                inc=1,
                device_id={"fsdp": ((chip + d) % pairs) * 2 + core},
                device_id_type=MESH,
            )
        pl.semaphore_signal(barrier, inc=1, device_id={"fsdp": partner}, device_id_type=MESH)
        waits += pairs
    pl.semaphore_wait(barrier, waits)

    def remote(src, dst, send, recv, where):
        return pltpu.make_async_remote_copy(
            src_ref=src,
            dst_ref=dst,
            send_sem=send,
            recv_sem=recv,
            device_id=where,
            device_id_type=MESH,
        )

    groups = {kind: [] for kind in EXTRA}
    for kind, src, dst in zip(kinds, ins, outs):
        groups[kind].append((src, dst, [rest.pop(0) for _ in range(EXTRA[kind])]))
    finish = []
    up = {"seq": lax.rem(z + 1, seq_n)}
    down = {"seq": lax.rem(z + seq_n - 1, seq_n)}
    has_up = z < seq_n - 1
    has_down = z > 0

    def line_start(dst, sems, src):
        up_send, up_recv, down_send, down_recv = sems

        @pl.when(has_up)
        def _():
            remote(src, dst.at[z], up_send.at[0], up_recv.at[1], up).start()

        @pl.when(has_down)
        def _():
            remote(src, dst.at[z], down_send.at[0], down_recv.at[1], down).start()

    def line_step(dst, sems, d):
        up_send, up_recv, down_send, down_recv = sems

        @pl.when(z >= d)
        def _():
            block = dst.at[lax.rem(z + seq_n - d, seq_n)]
            remote(block, block, up_send.at[d], up_recv.at[d], up).wait_recv()
            if d < seq_n - 1:

                @pl.when(has_up)
                def _():
                    remote(block, block, up_send.at[d], up_recv.at[d + 1], up).start()

        @pl.when(z + d < seq_n)
        def _():
            block = dst.at[lax.rem(z + d, seq_n)]
            remote(block, block, down_send.at[d], down_recv.at[d], down).wait_recv()
            if d < seq_n - 1:

                @pl.when(has_down)
                def _():
                    remote(block, block, down_send.at[d], down_recv.at[d + 1], down).start()

    def line_end(dst, sems, src):
        up_send, up_recv, down_send, down_recv = sems
        for d in range(seq_n - 1):

            @pl.when(jnp.logical_and(has_up, z >= d))
            def _():
                block = src if d == 0 else dst.at[lax.rem(z + seq_n - d, seq_n)]
                remote(block, dst.at[z], up_send.at[d], up_recv.at[d + 1], up).wait_send()

            @pl.when(jnp.logical_and(has_down, z + d < seq_n))
            def _():
                block = src if d == 0 else dst.at[lax.rem(z + d, seq_n)]
                remote(block, dst.at[z], down_send.at[d], down_recv.at[d + 1], down).wait_send()

    for src, dst, extra in groups["grad"]:
        held, total, send_a, recv_a, send_b, recv_b = extra[:6]
        for d in range(pairs):
            block = ((chip + d) % pairs) * 2
            remote(
                src.at[block + 1 - core], held.at[d], send_a.at[d], recv_a.at[d], {"fsdp": partner}
            ).start()
    for src, dst, extra in groups["fold"]:
        up_buf, up_sum, down_buf, down_sum, up_send, up_recv, down_send, down_recv = extra
        for k in range(seq_n - 1):
            t = seq_n - 1 - k

            @pl.when(z == 0)
            def _():
                remote(src.at[t], up_buf.at[t], up_send.at[t], up_recv.at[t], up).start()

            @pl.when(z == seq_n - 1)
            def _():
                remote(src.at[k], down_buf.at[k], down_send.at[k], down_recv.at[k], down).start()

    for src, dst, extra in groups["gather"]:
        line_start(dst, extra, src)
    for src, dst, extra in groups["swap"]:
        send, recv, own = extra
        for d in range(1, seq_n):
            to = (z + d) % seq_n
            piece = src.at[to]
            copy = remote(piece, dst.at[z], send.at[d], recv.at[d], {"seq": to})
            copy.start()
            finish.append(copy.wait_send)
            origin = (z + seq_n - d) % seq_n
            arrival = remote(piece, dst.at[origin], send.at[d], recv.at[d], {"seq": to})
            finish.append(arrival.wait_recv)
        local_copy = pltpu.make_async_copy(src.at[z], dst.at[z], own.at[0])
        local_copy.start()
        finish.append(local_copy.wait)
    for src, dst, extra in groups["spread"]:
        send_a, recv_a, send_b, recv_b, own = extra
        for d in range(1, pairs):
            copy = remote(
                src,
                dst.at[f],
                send_a.at[d],
                recv_a.at[d],
                {"fsdp": ((chip + d) % pairs) * 2 + core},
            )
            copy.start()
            finish.append(copy.wait_send)
        copy = remote(src, dst.at[f], send_b.at[0], recv_b.at[0], {"fsdp": partner})
        copy.start()
        finish.append(copy.wait_send)
        local_copy = pltpu.make_async_copy(src, dst.at[f], own.at[0])
        local_copy.start()
        finish.append(local_copy.wait)
    for src, dst, extra in groups["gather"]:
        dst[z] = src[...]
    for src, dst, extra in groups["grad"]:
        held, total, send_a, recv_a, send_b, recv_b = extra[:6]
        for d in list(range(1, pairs)) + [0]:
            block = ((chip + d) % pairs) * 2
            pair_copy = remote(
                src.at[block + 1 - core], held.at[d], send_a.at[d], recv_a.at[d], {"fsdp": partner}
            )
            pair_copy.wait_recv()
            finish.append(pair_copy.wait_send)
            total[d] = (src[block + core].astype(f32) + held[d].astype(f32)).astype(src.dtype)
            if d > 0:
                copy = remote(
                    total.at[d],
                    extra[10].at[d],
                    send_b.at[d],
                    recv_b.at[d],
                    {"fsdp": block + core},
                )
                copy.start()
                finish.append(copy.wait_send)
    for d in range(1, seq_n):
        for src, dst, extra in groups["gather"]:
            line_step(dst, extra, d)
        for src, dst, extra in groups["spread"]:
            send_a, recv_a, send_b, recv_b, own = extra
            for e in range(1, pairs):
                if e % (seq_n - 1) != d % (seq_n - 1):
                    continue
                origin = ((chip + pairs - e) % pairs) * 2 + core
                remote(src, dst.at[origin], send_a.at[e], recv_a.at[e], {"fsdp": partner}).wait_recv()
                copy = remote(
                    dst.at[origin], dst.at[origin], send_b.at[e], recv_b.at[e], {"fsdp": partner}
                )
                copy.start()
                finish.append(copy.wait_send)
        k = d - 1
        t = seq_n - 1 - k
        for src, dst, extra in groups["fold"]:
            up_buf, up_sum, down_buf, down_sum, up_send, up_recv, down_send, down_recv = extra

            @pl.when(jnp.logical_and(z > 0, z < t))
            def _():
                remote(src.at[t], up_buf.at[t], up_send.at[t], up_recv.at[t], up).wait_recv()
                up_sum[t] = (src[t].astype(f32) + up_buf[t].astype(f32)).astype(src.dtype)
                remote(up_sum.at[t], up_buf.at[t], up_send.at[t], up_recv.at[t], up).start()

            @pl.when(jnp.logical_and(z < seq_n - 1, z > k))
            def _():
                remote(src.at[k], down_buf.at[k], down_send.at[k], down_recv.at[k], down).wait_recv()
                down_sum[k] = (src[k].astype(f32) + down_buf[k].astype(f32)).astype(src.dtype)
                remote(down_sum.at[k], down_buf.at[k], down_send.at[k], down_recv.at[k], down).start()

    for src, dst, extra in groups["grad"]:
        held, total, send_a, recv_a, send_b, recv_b = extra[:6]
        value = total[0].astype(f32)
        for d in range(1, pairs):
            remote(
                total.at[d], extra[10].at[d], send_b.at[d], recv_b.at[d], {"fsdp": partner}
            ).wait_recv()
            value = value + extra[10][d].astype(f32)
        dst[z] = value.astype(src.dtype)
        line_start(dst, extra[6:10], dst.at[z])
    for d in range(1, seq_n):
        for src, dst, extra in groups["grad"]:
            line_step(dst, extra[6:10], d)
    for src, dst, extra in groups["fold"]:
        up_buf, up_sum, down_buf, down_sum, up_send, up_recv, down_send, down_recv = extra
        dst[...] = src[z].astype(f32)

        @pl.when(z > 0)
        def _():
            remote(src.at[z], up_buf.at[z], up_send.at[z], up_recv.at[z], up).wait_recv()
            dst[...] += up_buf[z].astype(f32)

        @pl.when(z < seq_n - 1)
        def _():
            remote(src.at[z], down_buf.at[z], down_send.at[z], down_recv.at[z], down).wait_recv()
            dst[...] += down_buf[z].astype(f32)

        for t in range(seq_n):

            @pl.when(z < t)
            def _():
                remote(src.at[t], up_buf.at[t], up_send.at[t], up_recv.at[t], up).wait_send()

            @pl.when(z > t)
            def _():
                remote(src.at[t], down_buf.at[t], down_send.at[t], down_recv.at[t], down).wait_send()

    for src, dst, extra in groups["spread"]:
        send_a, recv_a, send_b, recv_b, own = extra
        for d in range(pairs):
            origin = ((chip + pairs - d) % pairs) * 2 + 1 - core
            finish.append(
                remote(src, dst.at[origin], send_b.at[d], recv_b.at[d], {"fsdp": partner}).wait_recv
            )
    for wait in finish:
        wait()
    for src, dst, extra in groups["gather"]:
        line_end(dst, extra, src)
    for src, dst, extra in groups["grad"]:
        line_end(dst, extra[6:10], dst.at[z])


def exchange(kinds, arrays, collective_id):
    seq_n = lax.axis_size("seq")
    fsdp_n = lax.axis_size("fsdp")
    pairs = fsdp_n // 2
    results = []
    scratch = []
    dma = pltpu.SemaphoreType.DMA
    for kind, array in zip(kinds, arrays):
        dtype = array.dtype
        if kind == "gather":
            shape = (seq_n,) + array.shape
            scratch += [dma((seq_n,))] * 4
        elif kind == "swap":
            shape = array.shape
            scratch += [dma((seq_n,)), dma((seq_n,)), dma((1,))]
        elif kind == "fold":
            shape = array.shape[1:]
            scratch += [pltpu.VMEM(array.shape, dtype)] * 4 + [dma((seq_n,))] * 4
            dtype = jnp.float32
        elif kind == "spread":
            shape = (fsdp_n,) + array.shape
            scratch += [dma((pairs,))] * 4 + [dma((1,))]
        else:
            shape = (seq_n,) + array.shape[1:]
            half = pltpu.VMEM((pairs,) + array.shape[1:], dtype)
            scratch += [half] * 2 + [dma((pairs,))] * 4 + [dma((seq_n,))] * 4 + [half]
        results.append(jax.ShapeDtypeStruct(shape, dtype))
    space = pl.BlockSpec(memory_space=pltpu.VMEM)
    return pl.pallas_call(
        functools.partial(exchange_kernel, tuple(kinds), seq_n, fsdp_n),
        out_shape=results,
        in_specs=[space] * len(kinds),
        out_specs=[space] * len(kinds),
        scratch_shapes=scratch,
        compiler_params=pltpu.CompilerParams(collective_id=collective_id, has_side_effects=True),
        name=f"exchange_{collective_id}",
    )(*arrays)


def layer_norm(values, gain_vec):
    middle = jnp.mean(values, axis=-1, keepdims=True)
    centred = values - middle
    inverse = lax.rsqrt(jnp.mean(centred * centred, axis=-1, keepdims=True) + eps)
    scaled = centred * inverse
    return (scaled * gain_vec, scaled, inverse)


def norm_back(upstream, scaled, inverse, gain_vec):
    weighted = upstream * gain_vec
    return inverse * (
        weighted
        - jnp.mean(weighted, axis=-1, keepdims=True)
        - scaled * jnp.mean(weighted * scaled, axis=-1, keepdims=True)
    )


def rotary_tables(positions, head_size):
    half_dim = head_size // 2
    frequency = theta ** (-jnp.arange(half_dim, dtype=jnp.float32) / half_dim)
    angles = positions.astype(jnp.float32)[..., None] * frequency
    return (jnp.cos(angles), jnp.sin(angles))


def rotate(values, cosine_table, sine_table):
    half_dim = values.shape[-1] // 2
    first_half = values[..., :half_dim]
    second_half = values[..., half_dim:]
    return jnp.concatenate(
        [
            first_half * cosine_table - second_half * sine_table,
            second_half * cosine_table + first_half * sine_table,
        ],
        axis=-1,
    )


def gelu_slope(values):
    return (
        0.5 * (1.0 + lax.erf(values * 0.7071067811865476))
        + values * jnp.exp(-0.5 * values * values) * 0.3989422804014327
    )


def dot(left, right, left_dim=1, right_dim=0):
    return lax.dot_general(
        left, right, (((left_dim,), (right_dim,)), ((), ())), preferred_element_type=jnp.float32
    )


def local(
    tokens,
    positions,
    norm1_gain,
    qkv_weight,
    out_weight,
    norm2_gain,
    in_weight,
    down_weight,
    cotangent,
):
    f32 = jnp.float32
    low = jnp.bfloat16
    groups = lax.axis_size("seq")
    fsdp_n = lax.axis_size("fsdp")
    z = lax.axis_index("seq")
    seq_dev, span_len, width = tokens.shape
    rows = seq_dev * span_len
    length = span_len * groups
    local_heads = HEADS // groups
    group_width = local_heads * HEAD_DIM
    shard = qkv_weight.shape[0]
    ff = down_weight.shape[0]
    ff_part = ff // groups
    scale = HEAD_DIM ** (-0.5)

    qkv_part = lax.dynamic_index_in_dim(
        qkv_weight.reshape(shard, 3, groups, group_width), z, 2, keepdims=False
    ).reshape(shard, 3 * group_width)
    in_part = lax.dynamic_index_in_dim(
        in_weight.reshape(shard, 2, groups, ff_part), z, 2, keepdims=False
    ).reshape(shard, 2 * ff_part)
    down_part = lax.dynamic_slice_in_dim(down_weight, z * ff_part, ff_part, 0).T
    gains = jnp.stack([norm1_gain, norm2_gain])
    own_tokens = tokens.reshape(rows, width)
    own_cotangent = cotangent.reshape(rows, width)

    def whole(stack):
        w = stack.shape[-1]
        return jnp.swapaxes(stack.reshape(groups, seq_dev, span_len, w), 0, 1).reshape(
            seq_dev * length, w
        )

    def spans(full):
        w = full.shape[-1]
        return jnp.swapaxes(full.reshape(seq_dev, groups, span_len, w), 0, 1).reshape(
            groups, rows, w
        )

    all_tokens, all_cot, all_pos, w_qkv, w_out, w_in, w_down, all_gains = exchange(
        ["gather", "gather", "gather", "spread", "spread", "spread", "spread", "spread"],
        [own_tokens, own_cotangent, positions, qkv_part, out_weight, in_part, down_part, gains],
        0,
    )
    all_tokens = whole(all_tokens)
    all_cot = whole(all_cot)
    all_pos = jnp.swapaxes(all_pos, 0, 1).reshape(seq_dev, length)
    w_qkv = w_qkv.reshape(width, 3 * group_width)
    w_out = w_out.reshape(width, width)
    w_in = w_in.reshape(width, 2 * ff_part)
    w_down = w_down.reshape(width, ff_part)
    gain_one = all_gains[:, 0].reshape(width).astype(f32)
    gain_two = all_gains[:, 1].reshape(width).astype(f32)

    normed_one, scaled_full, _ = layer_norm(all_tokens.astype(f32), gain_one)
    normed_one = normed_one.astype(low)
    projected = dot(normed_one, w_qkv).reshape(seq_dev, length, 3, local_heads, HEAD_DIM)
    projected = projected.transpose(2, 0, 3, 1, 4)
    cosine, sine = rotary_tables(all_pos, HEAD_DIM)
    cosine = cosine[:, None]
    sine = sine[:, None]
    query = rotate(projected[0], cosine, sine).astype(low)
    key = rotate(projected[1], cosine, sine).astype(low)
    value = projected[2].astype(low)
    scores = jnp.einsum("bhqd,bhkd->bhqk", query, key, preferred_element_type=f32) * scale
    totals = jax.nn.logsumexp(scores, axis=-1, keepdims=True)
    probs = jnp.exp(scores - totals)
    probs_low = probs.astype(low)
    attended = jnp.einsum("bhqk,bhkd->bhqd", probs_low, value, preferred_element_type=f32).astype(
        low
    )

    def to_rows(heads):
        return heads.transpose(0, 2, 1, 3).reshape(seq_dev * length, group_width)

    (mixed,) = exchange(["swap"], [spans(to_rows(attended))], 1)
    mixed = jnp.swapaxes(mixed, 0, 1).reshape(rows, width)
    inputs = own_tokens.astype(f32)
    residual = inputs + dot(mixed, w_out)
    normed_two, scaled_two, inverse_two = layer_norm(residual, gain_two)
    normed_two = normed_two.astype(low)
    (normed_full,) = exchange(["gather"], [normed_two], 2)
    normed_full = whole(normed_full)
    lifted = dot(normed_full, w_in)
    act = lifted[:, :ff_part]
    gate = lifted[:, ff_part:]
    activated = jax.nn.gelu(act, approximate=False)
    gated = (activated * gate).astype(low)
    gated_grad = dot(all_cot, w_down)
    lifted_grad = jnp.concatenate(
        [gated_grad * gate * gelu_slope(act), gated_grad * activated], axis=1
    ).astype(low)
    ffn_part = dot(gated, w_down, 1, 1).astype(low)
    normed_grad_part = dot(lifted_grad, w_in, 1, 1).astype(low)
    ffn_parts, normed_grad_parts = exchange(
        ["fold", "fold"], [spans(ffn_part), spans(normed_grad_part)], 3
    )
    block_out = (residual + ffn_parts).astype(low)
    normed_two_grad = normed_grad_parts
    gain_two_grad = jnp.sum(normed_two_grad * scaled_two, axis=0)
    residual_grad = own_cotangent.astype(f32) + norm_back(
        normed_two_grad, scaled_two, inverse_two, gain_two
    )
    residual_low = residual_grad.astype(low)
    mixed_grad = dot(residual_low, w_out, 1, 1).astype(low)
    (head_grad,) = exchange(
        ["swap"], [jnp.swapaxes(mixed_grad.reshape(rows, groups, group_width), 0, 1)], 4
    )
    head_grad = whole(head_grad).reshape(seq_dev, length, local_heads, HEAD_DIM)
    head_grad = head_grad.transpose(0, 2, 1, 3)
    delta = jnp.sum(head_grad.astype(f32) * attended.astype(f32), axis=-1, keepdims=True)
    value_grad = jnp.einsum("bhqk,bhqd->bhkd", probs_low, head_grad, preferred_element_type=f32)
    prob_grad = jnp.einsum("bhqd,bhkd->bhqk", head_grad, value, preferred_element_type=f32)
    score_grad = (probs * (prob_grad - delta)).astype(low)
    query_grad = jnp.einsum("bhqk,bhkd->bhqd", score_grad, key, preferred_element_type=f32) * scale
    key_grad = jnp.einsum("bhqk,bhqd->bhkd", score_grad, query, preferred_element_type=f32) * scale
    qkv_grad = jnp.concatenate(
        [
            to_rows(rotate(query_grad.astype(low).astype(f32), cosine, -sine).astype(low)),
            to_rows(rotate(key_grad.astype(low).astype(f32), cosine, -sine).astype(low)),
            to_rows(value_grad.astype(low)),
        ],
        axis=1,
    )
    normed_one_grad_part = dot(qkv_grad, w_qkv, 1, 1)
    gain_one_grad = jnp.sum(normed_one_grad_part * scaled_full, axis=0)

    qkv_term = dot(normed_one, qkv_grad, 0, 0).astype(low)
    in_term = dot(normed_full, lifted_grad, 0, 0).astype(low)
    down_term = dot(all_cot, gated, 0, 0).astype(low)
    out_term = dot(mixed, residual_low, 0, 0).astype(low)
    gain_terms = jnp.stack(
        [gain_one_grad.reshape(fsdp_n, shard), gain_two_grad.reshape(fsdp_n, shard)], axis=1
    )
    parts = exchange(
        ["fold", "grad", "grad", "grad", "grad", "grad"],
        [spans(normed_one_grad_part.astype(low))]
        + [t.reshape(fsdp_n, shard, t.shape[1]) for t in (qkv_term, in_term, down_term, out_term)]
        + [gain_terms],
        5,
    )
    normed_one_grad = parts[0]
    _, scaled_one, inverse_one = layer_norm(inputs, gain_one)
    input_grad = (
        residual_grad + norm_back(normed_one_grad, scaled_one, inverse_one, gain_one)
    ).astype(low)
    qkv_all, in_all, down_all, out_all, gain_all = parts[1:]
    qkv_out = (
        qkv_all.reshape(groups, shard, 3, group_width)
        .transpose(1, 2, 0, 3)
        .reshape(shard, 3 * width)
        .astype(f32)
    )
    in_out = (
        in_all.reshape(groups, shard, 2, ff_part)
        .transpose(1, 2, 0, 3)
        .reshape(shard, 2 * ff)
        .astype(f32)
    )
    down_out = down_all.transpose(0, 2, 1).reshape(ff, shard).astype(f32)
    out_out = jnp.sum(out_all.astype(f32), axis=0)
    gain_out = jnp.sum(gain_all, axis=0)
    return (
        block_out.reshape(seq_dev, span_len, width),
        input_grad.reshape(seq_dev, span_len, width),
        qkv_out,
        out_out,
        in_out,
        down_out,
        gain_out[0],
        gain_out[1],
    )


def solution(mesh):
    in_specs = (
        P("fsdp", "seq", None),
        P("fsdp", "seq"),
        P("fsdp"),
        P("fsdp", None),
        P("fsdp", None),
        P("fsdp"),
        P("fsdp", None),
        P(None, "fsdp"),
        P("fsdp", "seq", None),
    )
    out_specs = (
        P("fsdp", "seq", None),
        P("fsdp", "seq", None),
        P("fsdp", None),
        P("fsdp", None),
        P("fsdp", None),
        P(None, "fsdp"),
        P("fsdp"),
        P("fsdp"),
    )
    return jax.shard_map(local, mesh=mesh, in_specs=in_specs, out_specs=out_specs, check_vma=False)
```

```python
import functools

import jax
import jax.numpy as jnp
from jax import lax
from jax.experimental import pallas as pl
from jax.experimental.pallas import tpu as pltpu
from jax.sharding import PartitionSpec as P

HEADS = 12
HEAD_DIM = 64
MESH = pl.DeviceIdType.MESH

eps = 1e-05
theta = 160000.0


EXTRA = {"gather": 4, "swap": 3, "spread": 5, "fold": 8, "grad": 11}


def exchange_kernel(kinds, seq_n, fsdp_n, *refs):
    f32 = jnp.float32
    count = len(kinds)
    ins = refs[:count]
    outs = refs[count : 2 * count]
    rest = list(refs[2 * count :])
    z = lax.axis_index("seq")
    f = lax.axis_index("fsdp")
    pairs = fsdp_n // 2
    chip = f // 2
    core = f % 2
    partner = chip * 2 + 1 - core
    on_seq = any(kind != "spread" for kind in kinds)
    on_fsdp = any(kind in ("spread", "grad") for kind in kinds)

    barrier = pltpu.get_barrier_semaphore()
    waits = 0
    if on_seq:
        for d in range(1, seq_n):
            pl.semaphore_signal(
                barrier, inc=1, device_id={"seq": (z + d) % seq_n}, device_id_type=MESH
            )
        waits += seq_n - 1
    if on_fsdp:
        for d in range(1, pairs):
            pl.semaphore_signal(
                barrier,
                inc=1,
                device_id={"fsdp": ((chip + d) % pairs) * 2 + core},
                device_id_type=MESH,
            )
        pl.semaphore_signal(barrier, inc=1, device_id={"fsdp": partner}, device_id_type=MESH)
        waits += pairs
    pl.semaphore_wait(barrier, waits)

    def remote(src, dst, send, recv, where):
        return pltpu.make_async_remote_copy(
            src_ref=src,
            dst_ref=dst,
            send_sem=send,
            recv_sem=recv,
            device_id=where,
            device_id_type=MESH,
        )

    groups = {kind: [] for kind in EXTRA}
    for kind, src, dst in zip(kinds, ins, outs):
        groups[kind].append((src, dst, [rest.pop(0) for _ in range(EXTRA[kind])]))
    finish = []
    up = {"seq": lax.rem(z + 1, seq_n)}
    down = {"seq": lax.rem(z + seq_n - 1, seq_n)}
    has_up = z < seq_n - 1
    has_down = z > 0

    def line_start(dst, sems, src):
        up_send, up_recv, down_send, down_recv = sems

        @pl.when(has_up)
        def _():
            remote(src, dst.at[z], up_send.at[0], up_recv.at[1], up).start()

        @pl.when(has_down)
        def _():
            remote(src, dst.at[z], down_send.at[0], down_recv.at[1], down).start()

    def line_step(dst, sems, d):
        up_send, up_recv, down_send, down_recv = sems

        @pl.when(z >= d)
        def _():
            block = dst.at[lax.rem(z + seq_n - d, seq_n)]
            remote(block, block, up_send.at[d], up_recv.at[d], up).wait_recv()
            if d < seq_n - 1:

                @pl.when(has_up)
                def _():
                    remote(block, block, up_send.at[d], up_recv.at[d + 1], up).start()

        @pl.when(z + d < seq_n)
        def _():
            block = dst.at[lax.rem(z + d, seq_n)]
            remote(block, block, down_send.at[d], down_recv.at[d], down).wait_recv()
            if d < seq_n - 1:

                @pl.when(has_down)
                def _():
                    remote(block, block, down_send.at[d], down_recv.at[d + 1], down).start()

    def line_end(dst, sems, src):
        up_send, up_recv, down_send, down_recv = sems
        for d in range(seq_n - 1):

            @pl.when(jnp.logical_and(has_up, z >= d))
            def _():
                block = src if d == 0 else dst.at[lax.rem(z + seq_n - d, seq_n)]
                remote(block, dst.at[z], up_send.at[d], up_recv.at[d + 1], up).wait_send()

            @pl.when(jnp.logical_and(has_down, z + d < seq_n))
            def _():
                block = src if d == 0 else dst.at[lax.rem(z + d, seq_n)]
                remote(block, dst.at[z], down_send.at[d], down_recv.at[d + 1], down).wait_send()

    for src, dst, extra in groups["grad"]:
        held, total, send_a, recv_a, send_b, recv_b = extra[:6]
        for d in range(pairs):
            block = ((chip + d) % pairs) * 2
            remote(
                src.at[block + 1 - core], held.at[d], send_a.at[d], recv_a.at[d], {"fsdp": partner}
            ).start()
    for k in range(seq_n - 1):
        t = seq_n - 1 - k
        for src, dst, extra in groups["fold"]:
            up_buf, up_sum, down_buf, down_sum, up_send, up_recv, down_send, down_recv = extra

            @pl.when(z == 0)
            def _():
                remote(src.at[t], up_buf.at[t], up_send.at[t], up_recv.at[t], up).start()

            @pl.when(z == seq_n - 1)
            def _():
                remote(src.at[k], down_buf.at[k], down_send.at[k], down_recv.at[k], down).start()

    for src, dst, extra in groups["gather"]:
        line_start(dst, extra, src)
    for src, dst, extra in groups["swap"]:
        send, recv, own = extra
        for d in range(1, seq_n):
            to = (z + d) % seq_n
            piece = src.at[to]
            copy = remote(piece, dst.at[z], send.at[d], recv.at[d], {"seq": to})
            copy.start()
            finish.append(copy.wait_send)
            origin = (z + seq_n - d) % seq_n
            arrival = remote(piece, dst.at[origin], send.at[d], recv.at[d], {"seq": to})
            finish.append(arrival.wait_recv)
        local_copy = pltpu.make_async_copy(src.at[z], dst.at[z], own.at[0])
        local_copy.start()
        finish.append(local_copy.wait)
    for src, dst, extra in groups["spread"]:
        send_a, recv_a, send_b, recv_b, own = extra
        for d in range(1, pairs):
            copy = remote(
                src,
                dst.at[f],
                send_a.at[d],
                recv_a.at[d],
                {"fsdp": ((chip + d) % pairs) * 2 + core},
            )
            copy.start()
            finish.append(copy.wait_send)
        copy = remote(src, dst.at[f], send_b.at[0], recv_b.at[0], {"fsdp": partner})
        copy.start()
        finish.append(copy.wait_send)
        local_copy = pltpu.make_async_copy(src, dst.at[f], own.at[0])
        local_copy.start()
        finish.append(local_copy.wait)
    for src, dst, extra in groups["gather"]:
        dst[z] = src[...]
    for src, dst, extra in groups["grad"]:
        held, total, send_a, recv_a, send_b, recv_b = extra[:6]
        for d in list(range(1, pairs)) + [0]:
            block = ((chip + d) % pairs) * 2
            pair_copy = remote(
                src.at[block + 1 - core], held.at[d], send_a.at[d], recv_a.at[d], {"fsdp": partner}
            )
            pair_copy.wait_recv()
            finish.append(pair_copy.wait_send)
            total[d] = (src[block + core].astype(f32) + held[d].astype(f32)).astype(src.dtype)
            if d > 0:
                copy = remote(
                    total.at[d],
                    extra[10].at[d],
                    send_b.at[d],
                    recv_b.at[d],
                    {"fsdp": block + core},
                )
                copy.start()
                finish.append(copy.wait_send)
    for d in range(1, seq_n):
        for src, dst, extra in groups["gather"]:
            line_step(dst, extra, d)
        for e in range(1, pairs) if d == max(seq_n - 2, 1) else ():
            for src, dst, extra in groups["spread"]:
                send_a, recv_a, send_b, recv_b, own = extra
                origin = ((chip + pairs - e) % pairs) * 2 + core
                remote(src, dst.at[origin], send_a.at[e], recv_a.at[e], {"fsdp": partner}).wait_recv()
                copy = remote(
                    dst.at[origin], dst.at[origin], send_b.at[e], recv_b.at[e], {"fsdp": partner}
                )
                copy.start()
                finish.append(copy.wait_send)
        k = d - 1
        t = seq_n - 1 - k
        for src, dst, extra in groups["fold"]:
            up_buf, up_sum, down_buf, down_sum, up_send, up_recv, down_send, down_recv = extra

            @pl.when(jnp.logical_and(z > 0, z < t))
            def _():
                remote(src.at[t], up_buf.at[t], up_send.at[t], up_recv.at[t], up).wait_recv()
                up_sum[t] = (src[t].astype(f32) + up_buf[t].astype(f32)).astype(src.dtype)
                remote(up_sum.at[t], up_buf.at[t], up_send.at[t], up_recv.at[t], up).start()

            @pl.when(jnp.logical_and(z < seq_n - 1, z > k))
            def _():
                remote(src.at[k], down_buf.at[k], down_send.at[k], down_recv.at[k], down).wait_recv()
                down_sum[k] = (src[k].astype(f32) + down_buf[k].astype(f32)).astype(src.dtype)
                remote(down_sum.at[k], down_buf.at[k], down_send.at[k], down_recv.at[k], down).start()

    for j in range(len(groups["grad"]) + seq_n - 1):
        for d in range(1, seq_n):
            if 0 <= j - d < len(groups["grad"]):
                line_step(groups["grad"][j - d][1], groups["grad"][j - d][2][6:10], d)
        if j >= len(groups["grad"]):
            continue
        src, dst, extra = groups["grad"][j]
        held, total, send_a, recv_a, send_b, recv_b = extra[:6]
        value = total[0].astype(f32)
        for d in range(1, pairs):
            remote(
                total.at[d], extra[10].at[d], send_b.at[d], recv_b.at[d], {"fsdp": partner}
            ).wait_recv()
            value = value + extra[10][d].astype(f32)
        dst[z] = value.astype(src.dtype)
        line_start(dst, extra[6:10], dst.at[z])
    for src, dst, extra in groups["fold"]:
        up_buf, up_sum, down_buf, down_sum, up_send, up_recv, down_send, down_recv = extra
        dst[...] = src[z].astype(f32)

        @pl.when(z > 0)
        def _():
            remote(src.at[z], up_buf.at[z], up_send.at[z], up_recv.at[z], up).wait_recv()
            dst[...] += up_buf[z].astype(f32)

        @pl.when(z < seq_n - 1)
        def _():
            remote(src.at[z], down_buf.at[z], down_send.at[z], down_recv.at[z], down).wait_recv()
            dst[...] += down_buf[z].astype(f32)

        for t in range(seq_n):

            @pl.when(z < t)
            def _():
                remote(src.at[t], up_buf.at[t], up_send.at[t], up_recv.at[t], up).wait_send()

            @pl.when(z > t)
            def _():
                remote(src.at[t], down_buf.at[t], down_send.at[t], down_recv.at[t], down).wait_send()

    for src, dst, extra in groups["spread"]:
        send_a, recv_a, send_b, recv_b, own = extra
        for d in range(pairs):
            origin = ((chip + pairs - d) % pairs) * 2 + 1 - core
            finish.append(
                remote(src, dst.at[origin], send_b.at[d], recv_b.at[d], {"fsdp": partner}).wait_recv
            )
    for wait in finish:
        wait()
    for src, dst, extra in groups["gather"]:
        line_end(dst, extra, src)
    for src, dst, extra in groups["grad"]:
        line_end(dst, extra[6:10], dst.at[z])


def exchange(kinds, arrays, collective_id):
    seq_n = lax.axis_size("seq")
    fsdp_n = lax.axis_size("fsdp")
    pairs = fsdp_n // 2
    results = []
    scratch = []
    dma = pltpu.SemaphoreType.DMA
    for kind, array in zip(kinds, arrays):
        dtype = array.dtype
        if kind == "gather":
            shape = (seq_n,) + array.shape
            scratch += [dma((seq_n,))] * 4
        elif kind == "swap":
            shape = array.shape
            scratch += [dma((seq_n,)), dma((seq_n,)), dma((1,))]
        elif kind == "fold":
            shape = array.shape[1:]
            scratch += [pltpu.VMEM(array.shape, dtype)] * 4 + [dma((seq_n,))] * 4
            dtype = jnp.float32
        elif kind == "spread":
            shape = (fsdp_n,) + array.shape
            scratch += [dma((pairs,))] * 4 + [dma((1,))]
        else:
            shape = (seq_n,) + array.shape[1:]
            half = pltpu.VMEM((pairs,) + array.shape[1:], dtype)
            scratch += [half] * 2 + [dma((pairs,))] * 4 + [dma((seq_n,))] * 4 + [half]
        results.append(jax.ShapeDtypeStruct(shape, dtype))
    space = pl.BlockSpec(memory_space=pltpu.VMEM)
    return pl.pallas_call(
        functools.partial(exchange_kernel, tuple(kinds), seq_n, fsdp_n),
        out_shape=results,
        in_specs=[space] * len(kinds),
        out_specs=[space] * len(kinds),
        scratch_shapes=scratch,
        compiler_params=pltpu.CompilerParams(collective_id=collective_id, has_side_effects=True),
        name=f"exchange_{collective_id}",
    )(*arrays)


def layer_norm(values, gain_vec):
    middle = jnp.mean(values, axis=-1, keepdims=True)
    centred = values - middle
    inverse = lax.rsqrt(jnp.mean(centred * centred, axis=-1, keepdims=True) + eps)
    scaled = centred * inverse
    return (scaled * gain_vec, scaled, inverse)


def norm_back(upstream, scaled, inverse, gain_vec):
    weighted = upstream * gain_vec
    return inverse * (
        weighted
        - jnp.mean(weighted, axis=-1, keepdims=True)
        - scaled * jnp.mean(weighted * scaled, axis=-1, keepdims=True)
    )


def rotary_tables(positions, head_size):
    half_dim = head_size // 2
    frequency = theta ** (-jnp.arange(half_dim, dtype=jnp.float32) / half_dim)
    angles = positions.astype(jnp.float32)[..., None] * frequency
    return (jnp.cos(angles), jnp.sin(angles))


def rotate(values, cosine_table, sine_table):
    half_dim = values.shape[-1] // 2
    first_half = values[..., :half_dim]
    second_half = values[..., half_dim:]
    return jnp.concatenate(
        [
            first_half * cosine_table - second_half * sine_table,
            second_half * cosine_table + first_half * sine_table,
        ],
        axis=-1,
    )


def gelu_slope(values):
    return (
        0.5 * (1.0 + lax.erf(values * 0.7071067811865476))
        + values * jnp.exp(-0.5 * values * values) * 0.3989422804014327
    )


def dot(left, right, left_dim=1, right_dim=0):
    return lax.dot_general(
        left, right, (((left_dim,), (right_dim,)), ((), ())), preferred_element_type=jnp.float32
    )


def local(
    tokens,
    positions,
    norm1_gain,
    qkv_weight,
    out_weight,
    norm2_gain,
    in_weight,
    down_weight,
    cotangent,
):
    f32 = jnp.float32
    low = jnp.bfloat16
    groups = lax.axis_size("seq")
    fsdp_n = lax.axis_size("fsdp")
    z = lax.axis_index("seq")
    seq_dev, span_len, width = tokens.shape
    rows = seq_dev * span_len
    length = span_len * groups
    local_heads = HEADS // groups
    group_width = local_heads * HEAD_DIM
    shard = qkv_weight.shape[0]
    ff = down_weight.shape[0]
    ff_part = ff // groups
    scale = HEAD_DIM ** (-0.5)

    def pick(weight, sections, section):
        part = None
        for g in range(groups):
            columns = [
                weight[:, (j * groups + g) * section : (j * groups + g + 1) * section]
                for j in range(sections)
            ]
            own = jnp.concatenate(columns, axis=1)
            part = own if part is None else jnp.where(z == g, own, part)
        return part

    qkv_part = pick(qkv_weight, 3, group_width)
    in_part = pick(in_weight, 2, ff_part)
    down_part = lax.dynamic_slice_in_dim(down_weight, z * ff_part, ff_part, 0).T
    gains = jnp.stack([norm1_gain, norm2_gain])
    own_tokens = tokens.reshape(rows, width)
    own_cotangent = cotangent.reshape(rows, width)

    def whole(stack):
        w = stack.shape[-1]
        return jnp.swapaxes(stack.reshape(groups, seq_dev, span_len, w), 0, 1).reshape(
            seq_dev * length, w
        )

    def spans(full):
        w = full.shape[-1]
        return jnp.swapaxes(full.reshape(seq_dev, groups, span_len, w), 0, 1).reshape(
            groups, rows, w
        )

    all_tokens, all_cot, all_pos, w_qkv, w_out, w_in, w_down, all_gains = exchange(
        ["gather", "gather", "gather", "spread", "spread", "spread", "spread", "spread"],
        [own_tokens, own_cotangent, positions, qkv_part, out_weight, in_part, down_part, gains],
        0,
    )
    all_tokens = whole(all_tokens)
    all_cot = whole(all_cot)
    all_pos = jnp.swapaxes(all_pos, 0, 1).reshape(seq_dev, length)
    w_qkv = w_qkv.reshape(width, 3 * group_width)
    w_out = w_out.reshape(width, width)
    w_in = w_in.reshape(width, 2 * ff_part)
    w_down = w_down.reshape(width, ff_part)
    gain_one = all_gains[:, 0].reshape(width).astype(f32)
    gain_two = all_gains[:, 1].reshape(width).astype(f32)

    normed_one, scaled_full, _ = layer_norm(all_tokens.astype(f32), gain_one)
    normed_one = normed_one.astype(low)
    projected = dot(normed_one, w_qkv).reshape(seq_dev, length, 3, local_heads, HEAD_DIM)
    projected = projected.transpose(2, 0, 3, 1, 4)
    cosine, sine = rotary_tables(all_pos, HEAD_DIM)
    cosine = cosine[:, None]
    sine = sine[:, None]
    query = rotate(projected[0], cosine, sine).astype(low)
    key = rotate(projected[1], cosine, sine).astype(low)
    value = projected[2].astype(low)
    scores = jnp.einsum("bhqd,bhkd->bhqk", query, key, preferred_element_type=f32) * scale
    totals = jax.nn.logsumexp(scores, axis=-1, keepdims=True)
    probs = jnp.exp(scores - totals)
    probs_low = probs.astype(low)
    attended = jnp.einsum("bhqk,bhkd->bhqd", probs_low, value, preferred_element_type=f32).astype(
        low
    )

    def to_rows(heads):
        return jnp.concatenate([heads[:, h] for h in range(local_heads)], axis=-1).reshape(
            seq_dev * length, group_width
        )

    (mixed,) = exchange(["swap"], [spans(to_rows(attended))], 1)
    w_out = w_out.reshape(groups, group_width, width)
    inputs = own_tokens.astype(f32)
    residual = inputs + jnp.einsum("grd,gdw->rw", mixed, w_out, preferred_element_type=f32)
    normed_two, scaled_two, inverse_two = layer_norm(residual, gain_two)
    normed_two = normed_two.astype(low)
    (normed_full,) = exchange(["gather"], [normed_two], 2)
    normed_full = whole(normed_full)
    lifted = dot(normed_full, w_in)
    act = lifted[:, :ff_part]
    gate = lifted[:, ff_part:]
    activated = jax.nn.gelu(act, approximate=False)
    gated = (activated * gate).astype(low)
    gated_grad = dot(all_cot, w_down)
    lifted_grad = jnp.concatenate(
        [gated_grad * gate * gelu_slope(act), gated_grad * activated], axis=1
    ).astype(low)
    ffn_part = dot(gated, w_down, 1, 1).astype(low)
    normed_grad_part = dot(lifted_grad, w_in, 1, 1).astype(low)
    (normed_two_grad,) = exchange(["fold"], [spans(normed_grad_part)], 3)
    gain_two_grad = jnp.sum(normed_two_grad * scaled_two, axis=0)
    residual_grad = own_cotangent.astype(f32) + norm_back(
        normed_two_grad, scaled_two, inverse_two, gain_two
    )
    residual_low = residual_grad.astype(low)
    mixed_grad = jnp.einsum("rw,gdw->grd", residual_low, w_out, preferred_element_type=f32)
    (head_grad,) = exchange(["swap"], [mixed_grad.astype(low)], 4)
    head_grad = whole(head_grad).reshape(seq_dev, length, local_heads, HEAD_DIM)
    head_grad = head_grad.transpose(0, 2, 1, 3)
    delta = jnp.sum(head_grad.astype(f32) * attended.astype(f32), axis=-1, keepdims=True)
    value_grad = jnp.einsum("bhqk,bhqd->bhkd", probs_low, head_grad, preferred_element_type=f32)
    prob_grad = jnp.einsum("bhqd,bhkd->bhqk", head_grad, value, preferred_element_type=f32)
    score_grad = (probs * (prob_grad - delta)).astype(low)
    query_grad = jnp.einsum("bhqk,bhkd->bhqd", score_grad, key, preferred_element_type=f32) * scale
    key_grad = jnp.einsum("bhqk,bhqd->bhkd", score_grad, query, preferred_element_type=f32) * scale
    qkv_grad = jnp.concatenate(
        [
            to_rows(rotate(query_grad.astype(low).astype(f32), cosine, -sine).astype(low)),
            to_rows(rotate(key_grad.astype(low).astype(f32), cosine, -sine).astype(low)),
            to_rows(value_grad.astype(low)),
        ],
        axis=1,
    )
    normed_one_grad_part = dot(qkv_grad, w_qkv, 1, 1)
    gain_one_grad = jnp.sum(normed_one_grad_part * scaled_full, axis=0)

    qkv_term = dot(normed_one, qkv_grad, 0, 0).astype(low)
    in_term = dot(normed_full, lifted_grad, 0, 0).astype(low)
    down_term = dot(all_cot, gated, 0, 0).astype(low)
    out_term = jnp.einsum("grd,rw->gdw", mixed, residual_low, preferred_element_type=f32)
    out_term = out_term.astype(low).reshape(width, width)
    gain_terms = jnp.stack(
        [gain_one_grad.reshape(fsdp_n, shard), gain_two_grad.reshape(fsdp_n, shard)], axis=1
    )
    parts = exchange(
        ["fold", "fold", "grad", "grad", "grad", "grad", "grad"],
        [spans(normed_one_grad_part.astype(low)), spans(ffn_part)]
        + [t.reshape(fsdp_n, shard, t.shape[1]) for t in (qkv_term, in_term, down_term, out_term)]
        + [gain_terms],
        5,
    )
    normed_one_grad = parts[0]
    _, scaled_one, inverse_one = layer_norm(inputs, gain_one)
    input_grad = (
        residual_grad + norm_back(normed_one_grad, scaled_one, inverse_one, gain_one)
    ).astype(low)
    block_out = (residual + parts[1]).astype(low)
    qkv_all, in_all, down_all, out_all, gain_all = parts[2:]

    def columns_of(stack, sections, section):
        return jnp.concatenate(
            [
                stack[g][:, j * section : (j + 1) * section]
                for j in range(sections)
                for g in range(groups)
            ],
            axis=1,
        ).astype(f32)

    qkv_out = columns_of(qkv_all, 3, group_width)
    in_out = columns_of(in_all, 2, ff_part)
    down_out = down_all.transpose(0, 2, 1).reshape(ff, shard).astype(f32)
    out_out = jnp.sum(out_all.astype(f32), axis=0)
    gain_out = jnp.sum(gain_all, axis=0)
    return (
        block_out.reshape(seq_dev, span_len, width),
        input_grad.reshape(seq_dev, span_len, width),
        qkv_out,
        out_out,
        in_out,
        down_out,
        gain_out[0],
        gain_out[1],
    )


def solution(mesh):
    in_specs = (
        P("fsdp", "seq", None),
        P("fsdp", "seq"),
        P("fsdp"),
        P("fsdp", None),
        P("fsdp", None),
        P("fsdp"),
        P("fsdp", None),
        P(None, "fsdp"),
        P("fsdp", "seq", None),
    )
    out_specs = (
        P("fsdp", "seq", None),
        P("fsdp", "seq", None),
        P("fsdp", None),
        P("fsdp", None),
        P("fsdp", None),
        P(None, "fsdp"),
        P("fsdp"),
        P("fsdp"),
    )
    return jax.shard_map(local, mesh=mesh, in_specs=in_specs, out_specs=out_specs, check_vma=False)
```

```python
import functools

import jax
import jax.numpy as jnp
from jax import lax
from jax.experimental import pallas as pl
from jax.experimental.pallas import tpu as pltpu
from jax.sharding import PartitionSpec as P

HEADS = 12
HEAD_DIM = 64
MESH = pl.DeviceIdType.MESH

eps = 1e-05
theta = 160000.0


EXTRA = {"gather": 4, "swap": 3, "spread": 5, "fold": 8, "grad": 11, "reduce": 11}


def exchange_kernel(kinds, seq_n, fsdp_n, *refs):
    f32 = jnp.float32
    count = len(kinds)
    ins = refs[:count]
    outs = refs[count : 2 * count]
    rest = list(refs[2 * count :])
    z = lax.axis_index("seq")
    f = lax.axis_index("fsdp")
    pairs = fsdp_n // 2
    chip = f // 2
    core = f % 2
    partner = chip * 2 + 1 - core
    on_seq = any(kind not in ("spread", "reduce") for kind in kinds)
    on_fsdp = any(kind in ("spread", "grad", "reduce") for kind in kinds)

    barrier = pltpu.get_barrier_semaphore()
    waits = 0
    if on_seq:
        for d in range(1, seq_n):
            pl.semaphore_signal(
                barrier, inc=1, device_id={"seq": (z + d) % seq_n}, device_id_type=MESH
            )
        waits += seq_n - 1
    if on_fsdp:
        for d in range(1, pairs):
            pl.semaphore_signal(
                barrier,
                inc=1,
                device_id={"fsdp": ((chip + d) % pairs) * 2 + core},
                device_id_type=MESH,
            )
        pl.semaphore_signal(barrier, inc=1, device_id={"fsdp": partner}, device_id_type=MESH)
        waits += pairs
    pl.semaphore_wait(barrier, waits)

    def remote(src, dst, send, recv, where):
        return pltpu.make_async_remote_copy(
            src_ref=src,
            dst_ref=dst,
            send_sem=send,
            recv_sem=recv,
            device_id=where,
            device_id_type=MESH,
        )

    groups = {kind: [] for kind in EXTRA}
    for kind, src, dst in zip(kinds, ins, outs):
        groups[kind].append((src, dst, [rest.pop(0) for _ in range(EXTRA[kind])]))
    finish = []
    up = {"seq": lax.rem(z + 1, seq_n)}
    down = {"seq": lax.rem(z + seq_n - 1, seq_n)}
    has_up = z < seq_n - 1
    has_down = z > 0

    def line_start(dst, sems, src):
        up_send, up_recv, down_send, down_recv = sems

        @pl.when(has_up)
        def _():
            remote(src, dst.at[z], up_send.at[0], up_recv.at[1], up).start()

        @pl.when(has_down)
        def _():
            remote(src, dst.at[z], down_send.at[0], down_recv.at[1], down).start()

    def line_step(dst, sems, d):
        up_send, up_recv, down_send, down_recv = sems

        @pl.when(z >= d)
        def _():
            block = dst.at[lax.rem(z + seq_n - d, seq_n)]
            remote(block, block, up_send.at[d], up_recv.at[d], up).wait_recv()
            if d < seq_n - 1:

                @pl.when(has_up)
                def _():
                    remote(block, block, up_send.at[d], up_recv.at[d + 1], up).start()

        @pl.when(z + d < seq_n)
        def _():
            block = dst.at[lax.rem(z + d, seq_n)]
            remote(block, block, down_send.at[d], down_recv.at[d], down).wait_recv()
            if d < seq_n - 1:

                @pl.when(has_down)
                def _():
                    remote(block, block, down_send.at[d], down_recv.at[d + 1], down).start()

    def line_end(dst, sems, src):
        up_send, up_recv, down_send, down_recv = sems
        for d in range(seq_n - 1):

            @pl.when(jnp.logical_and(has_up, z >= d))
            def _():
                block = src if d == 0 else dst.at[lax.rem(z + seq_n - d, seq_n)]
                remote(block, dst.at[z], up_send.at[d], up_recv.at[d + 1], up).wait_send()

            @pl.when(jnp.logical_and(has_down, z + d < seq_n))
            def _():
                block = src if d == 0 else dst.at[lax.rem(z + d, seq_n)]
                remote(block, dst.at[z], down_send.at[d], down_recv.at[d + 1], down).wait_send()

    lower = z * 2 < seq_n

    def fold_steps(k, first):
        t = seq_n - 1 - k
        for src, dst, extra in groups["fold"]:
            up_buf, up_sum, down_buf, down_sum, up_send, up_recv, down_send, down_recv = extra
            near_up = lower if first else jnp.logical_not(lower)

            @pl.when(jnp.logical_and(near_up, jnp.logical_and(z > 0, z < t)))
            def _():
                remote(src.at[t], up_buf.at[t], up_send.at[t], up_recv.at[t], up).wait_recv()
                up_sum[t] = (src[t].astype(f32) + up_buf[t].astype(f32)).astype(src.dtype)
                remote(up_sum.at[t], up_buf.at[t], up_send.at[t], up_recv.at[t], up).start()

            @pl.when(
                jnp.logical_and(
                    jnp.logical_not(near_up), jnp.logical_and(z < seq_n - 1, z > k)
                )
            )
            def _():
                remote(src.at[k], down_buf.at[k], down_send.at[k], down_recv.at[k], down).wait_recv()
                down_sum[k] = (src[k].astype(f32) + down_buf[k].astype(f32)).astype(src.dtype)
                remote(down_sum.at[k], down_buf.at[k], down_send.at[k], down_recv.at[k], down).start()

    for src, dst, extra in groups["grad"] + groups["reduce"]:
        held, total, send_a, recv_a, send_b, recv_b = extra[:6]
        for d in range(pairs):
            block = ((chip + d) % pairs) * 2
            remote(
                src.at[block + 1 - core], held.at[d], send_a.at[d], recv_a.at[d], {"fsdp": partner}
            ).start()
    for src, dst, extra in groups["gather"]:
        line_start(dst, extra, src)
    for k in range(seq_n - 1):
        t = seq_n - 1 - k
        for src, dst, extra in groups["fold"]:
            up_buf, up_sum, down_buf, down_sum, up_send, up_recv, down_send, down_recv = extra

            @pl.when(z == 0)
            def _():
                remote(src.at[t], up_buf.at[t], up_send.at[t], up_recv.at[t], up).start()

            @pl.when(z == seq_n - 1)
            def _():
                remote(src.at[k], down_buf.at[k], down_send.at[k], down_recv.at[k], down).start()

    for src, dst, extra in groups["swap"]:
        send, recv, own = extra
        for d in range(1, seq_n):
            to = (z + d) % seq_n
            piece = src.at[to]
            copy = remote(piece, dst.at[z], send.at[d], recv.at[d], {"seq": to})
            copy.start()
            finish.append(copy.wait_send)
            origin = (z + seq_n - d) % seq_n
            arrival = remote(piece, dst.at[origin], send.at[d], recv.at[d], {"seq": to})
            finish.append(arrival.wait_recv)
        local_copy = pltpu.make_async_copy(src.at[z], dst.at[z], own.at[0])
        local_copy.start()
        finish.append(local_copy.wait)
    for src, dst, extra in groups["spread"]:
        send_a, recv_a, send_b, recv_b, own = extra
        for d in range(1, pairs):
            copy = remote(
                src,
                dst.at[f],
                send_a.at[d],
                recv_a.at[d],
                {"fsdp": ((chip + d) % pairs) * 2 + core},
            )
            copy.start()
            finish.append(copy.wait_send)
        copy = remote(src, dst.at[f], send_b.at[0], recv_b.at[0], {"fsdp": partner})
        copy.start()
        finish.append(copy.wait_send)
        local_copy = pltpu.make_async_copy(src, dst.at[f], own.at[0])
        local_copy.start()
        finish.append(local_copy.wait)
    for src, dst, extra in groups["gather"]:
        dst[z] = src[...]
    for src, dst, extra in groups["grad"] + groups["reduce"]:
        held, total, send_a, recv_a, send_b, recv_b = extra[:6]
        for d in list(range(1, pairs)) + [0]:
            block = ((chip + d) % pairs) * 2
            pair_copy = remote(
                src.at[block + 1 - core], held.at[d], send_a.at[d], recv_a.at[d], {"fsdp": partner}
            )
            pair_copy.wait_recv()
            finish.append(pair_copy.wait_send)
            total[d] = (src[block + core].astype(f32) + held[d].astype(f32)).astype(src.dtype)
            if d > 0:
                copy = remote(
                    total.at[d],
                    extra[10].at[d],
                    send_b.at[d],
                    recv_b.at[d],
                    {"fsdp": block + core},
                )
                copy.start()
                finish.append(copy.wait_send)
    for d in range(1, seq_n):
        for src, dst, extra in groups["gather"]:
            line_step(dst, extra, d)
        for e in range(1, pairs) if d == max(seq_n - 2, 1) else ():
            for src, dst, extra in groups["spread"]:
                send_a, recv_a, send_b, recv_b, own = extra
                origin = ((chip + pairs - e) % pairs) * 2 + core
                remote(src, dst.at[origin], send_a.at[e], recv_a.at[e], {"fsdp": partner}).wait_recv()
                copy = remote(
                    dst.at[origin], dst.at[origin], send_b.at[e], recv_b.at[e], {"fsdp": partner}
                )
                copy.start()
                finish.append(copy.wait_send)
        fold_steps(d - 1, True)
    for k in range(seq_n - 1):
        fold_steps(k, False)

    for j in range(len(groups["grad"]) + seq_n - 1):
        for d in range(1, seq_n):
            if 0 <= j - d < len(groups["grad"]):
                line_step(groups["grad"][j - d][1], groups["grad"][j - d][2][6:10], d)
        if j >= len(groups["grad"]):
            continue
        src, dst, extra = groups["grad"][j]
        held, total, send_a, recv_a, send_b, recv_b = extra[:6]
        value = total[0].astype(f32)
        for d in range(1, pairs):
            remote(
                total.at[d], extra[10].at[d], send_b.at[d], recv_b.at[d], {"fsdp": partner}
            ).wait_recv()
            value = value + extra[10][d].astype(f32)
        dst[z] = value.astype(src.dtype)
        line_start(dst, extra[6:10], dst.at[z])
    for src, dst, extra in groups["reduce"]:
        total, send_b, recv_b = extra[1], extra[4], extra[5]
        value = total[0].astype(f32)
        for d in range(1, pairs):
            remote(
                total.at[d], extra[10].at[d], send_b.at[d], recv_b.at[d], {"fsdp": partner}
            ).wait_recv()
            value = value + extra[10][d].astype(f32)
        dst[...] = value.astype(src.dtype)
    for src, dst, extra in groups["fold"]:
        up_buf, up_sum, down_buf, down_sum, up_send, up_recv, down_send, down_recv = extra
        dst[...] = src[z].astype(f32)

        @pl.when(z > 0)
        def _():
            remote(src.at[z], up_buf.at[z], up_send.at[z], up_recv.at[z], up).wait_recv()
            dst[...] += up_buf[z].astype(f32)

        @pl.when(z < seq_n - 1)
        def _():
            remote(src.at[z], down_buf.at[z], down_send.at[z], down_recv.at[z], down).wait_recv()
            dst[...] += down_buf[z].astype(f32)

        for t in range(seq_n):

            @pl.when(z < t)
            def _():
                remote(src.at[t], up_buf.at[t], up_send.at[t], up_recv.at[t], up).wait_send()

            @pl.when(z > t)
            def _():
                remote(src.at[t], down_buf.at[t], down_send.at[t], down_recv.at[t], down).wait_send()

    for src, dst, extra in groups["spread"]:
        send_a, recv_a, send_b, recv_b, own = extra
        for d in range(pairs):
            origin = ((chip + pairs - d) % pairs) * 2 + 1 - core
            finish.append(
                remote(src, dst.at[origin], send_b.at[d], recv_b.at[d], {"fsdp": partner}).wait_recv
            )
    for wait in finish:
        wait()
    for src, dst, extra in groups["gather"]:
        line_end(dst, extra, src)
    for src, dst, extra in groups["grad"]:
        line_end(dst, extra[6:10], dst.at[z])


def exchange(kinds, arrays, collective_id):
    seq_n = lax.axis_size("seq")
    fsdp_n = lax.axis_size("fsdp")
    pairs = fsdp_n // 2
    results = []
    scratch = []
    dma = pltpu.SemaphoreType.DMA
    for kind, array in zip(kinds, arrays):
        dtype = array.dtype
        if kind == "gather":
            shape = (seq_n,) + array.shape
            scratch += [dma((seq_n,))] * 4
        elif kind == "swap":
            shape = array.shape
            scratch += [dma((seq_n,)), dma((seq_n,)), dma((1,))]
        elif kind == "fold":
            shape = array.shape[1:]
            scratch += [pltpu.VMEM(array.shape, dtype)] * 4 + [dma((seq_n,))] * 4
            dtype = jnp.float32
        elif kind == "spread":
            shape = (fsdp_n,) + array.shape
            scratch += [dma((pairs,))] * 4 + [dma((1,))]
        else:
            shape = array.shape[1:]
            if kind == "grad":
                shape = (seq_n,) + shape
            half = pltpu.VMEM((pairs,) + array.shape[1:], dtype)
            scratch += [half] * 2 + [dma((pairs,))] * 4 + [dma((seq_n,))] * 4 + [half]
        results.append(jax.ShapeDtypeStruct(shape, dtype))
    space = pl.BlockSpec(memory_space=pltpu.VMEM)
    return pl.pallas_call(
        functools.partial(exchange_kernel, tuple(kinds), seq_n, fsdp_n),
        out_shape=results,
        in_specs=[space] * len(kinds),
        out_specs=[space] * len(kinds),
        scratch_shapes=scratch,
        compiler_params=pltpu.CompilerParams(collective_id=collective_id, has_side_effects=True),
        name=f"exchange_{collective_id}",
    )(*arrays)


def layer_norm(values, gain_vec):
    middle = jnp.mean(values, axis=-1, keepdims=True)
    centred = values - middle
    inverse = lax.rsqrt(jnp.mean(centred * centred, axis=-1, keepdims=True) + eps)
    scaled = centred * inverse
    return (scaled * gain_vec, scaled, inverse)


def norm_back(upstream, scaled, inverse, gain_vec):
    weighted = upstream * gain_vec
    return inverse * (
        weighted
        - jnp.mean(weighted, axis=-1, keepdims=True)
        - scaled * jnp.mean(weighted * scaled, axis=-1, keepdims=True)
    )


def rotary_tables(positions, head_size):
    half_dim = head_size // 2
    frequency = theta ** (-jnp.arange(half_dim, dtype=jnp.float32) / half_dim)
    angles = positions.astype(jnp.float32)[..., None] * frequency
    return (jnp.cos(angles), jnp.sin(angles))


def rotate(values, cosine_table, sine_table):
    half_dim = values.shape[-1] // 2
    first_half = values[..., :half_dim]
    second_half = values[..., half_dim:]
    return jnp.concatenate(
        [
            first_half * cosine_table - second_half * sine_table,
            second_half * cosine_table + first_half * sine_table,
        ],
        axis=-1,
    )


def gelu_slope(values):
    return (
        0.5 * (1.0 + lax.erf(values * 0.7071067811865476))
        + values * jnp.exp(-0.5 * values * values) * 0.3989422804014327
    )


def dot(left, right, left_dim=1, right_dim=0):
    return lax.dot_general(
        left, right, (((left_dim,), (right_dim,)), ((), ())), preferred_element_type=jnp.float32
    )


def local(
    tokens,
    positions,
    norm1_gain,
    qkv_weight,
    out_weight,
    norm2_gain,
    in_weight,
    down_weight,
    cotangent,
):
    f32 = jnp.float32
    low = jnp.bfloat16
    groups = lax.axis_size("seq")
    fsdp_n = lax.axis_size("fsdp")
    z = lax.axis_index("seq")
    seq_dev, span_len, width = tokens.shape
    rows = seq_dev * span_len
    length = span_len * groups
    local_heads = HEADS // groups
    group_width = local_heads * HEAD_DIM
    shard = qkv_weight.shape[0]
    ff = down_weight.shape[0]
    ff_part = ff // groups
    scale = HEAD_DIM ** (-0.5)

    def pick(weight, sections, section):
        part = None
        for g in range(groups):
            columns = [
                weight[:, (j * groups + g) * section : (j * groups + g + 1) * section]
                for j in range(sections)
            ]
            own = jnp.concatenate(columns, axis=1)
            part = own if part is None else jnp.where(z == g, own, part)
        return part

    qkv_part = pick(qkv_weight, 3, group_width)
    in_part = pick(in_weight, 2, ff_part)
    down_part = lax.dynamic_slice_in_dim(down_weight, z * ff_part, ff_part, 0).T
    gains = jnp.stack([norm1_gain, norm2_gain])
    own_tokens = tokens.reshape(rows, width)
    own_cotangent = cotangent.reshape(rows, width)

    def whole(stack):
        w = stack.shape[-1]
        return jnp.swapaxes(stack.reshape(groups, seq_dev, span_len, w), 0, 1).reshape(
            seq_dev * length, w
        )

    def spans(full):
        w = full.shape[-1]
        return jnp.swapaxes(full.reshape(seq_dev, groups, span_len, w), 0, 1).reshape(
            groups, rows, w
        )

    all_tokens, all_cot, all_pos, w_qkv, w_out, w_in, w_down, all_gains = exchange(
        ["gather", "gather", "gather", "spread", "spread", "spread", "spread", "spread"],
        [own_tokens, own_cotangent, positions, qkv_part, out_weight, in_part, down_part, gains],
        0,
    )
    all_tokens = whole(all_tokens)
    all_cot = whole(all_cot)
    all_pos = jnp.swapaxes(all_pos, 0, 1).reshape(seq_dev, length)
    w_qkv = w_qkv.reshape(width, 3 * group_width)
    w_out = w_out.reshape(width, width)
    w_in = w_in.reshape(width, 2 * ff_part)
    w_down = w_down.reshape(width, ff_part)
    gain_one = all_gains[:, 0].reshape(width).astype(f32)
    gain_two = all_gains[:, 1].reshape(width).astype(f32)

    normed_one, scaled_full, _ = layer_norm(all_tokens.astype(f32), gain_one)
    normed_one = normed_one.astype(low)
    projected = dot(normed_one, w_qkv).reshape(seq_dev, length, 3, local_heads, HEAD_DIM)
    projected = projected.transpose(2, 0, 3, 1, 4)
    cosine, sine = rotary_tables(all_pos, HEAD_DIM)
    cosine = cosine[:, None]
    sine = sine[:, None]
    query = rotate(projected[0], cosine, sine).astype(low)
    key = rotate(projected[1], cosine, sine).astype(low)
    value = projected[2].astype(low)
    scores = jnp.einsum("bhqd,bhkd->bhqk", query, key, preferred_element_type=f32) * scale
    totals = jax.nn.logsumexp(scores, axis=-1, keepdims=True)
    probs = jnp.exp(scores - totals)
    probs_low = probs.astype(low)
    attended = jnp.einsum("bhqk,bhkd->bhqd", probs_low, value, preferred_element_type=f32).astype(
        low
    )

    def to_rows(heads):
        return jnp.concatenate([heads[:, h] for h in range(local_heads)], axis=-1).reshape(
            seq_dev * length, group_width
        )

    (mixed,) = exchange(["swap"], [spans(to_rows(attended))], 1)
    w_out = w_out.reshape(groups, group_width, width)
    inputs = own_tokens.astype(f32)
    residual = inputs + jnp.einsum("grd,gdw->rw", mixed, w_out, preferred_element_type=f32)
    normed_two, scaled_two, inverse_two = layer_norm(residual, gain_two)
    normed_two = normed_two.astype(low)
    (normed_full,) = exchange(["gather"], [normed_two], 2)
    normed_full = whole(normed_full)
    lifted = dot(normed_full, w_in)
    act = lifted[:, :ff_part]
    gate = lifted[:, ff_part:]
    activated = jax.nn.gelu(act, approximate=False)
    gated = (activated * gate).astype(low)
    gated_grad = dot(all_cot, w_down)
    lifted_grad = jnp.concatenate(
        [gated_grad * gate * gelu_slope(act), gated_grad * activated], axis=1
    ).astype(low)
    ffn_part = dot(gated, w_down, 1, 1).astype(low)
    normed_grad_part = dot(lifted_grad, w_in, 1, 1).astype(low)
    in_term = dot(normed_full, lifted_grad, 0, 0).astype(low)
    down_term = dot(all_cot, gated, 0, 0).astype(low)

    def by_owner(term):
        return term.reshape(fsdp_n, shard, term.shape[1])

    normed_two_grad, in_owned, down_owned = exchange(
        ["fold", "reduce", "reduce"],
        [spans(normed_grad_part), by_owner(in_term), by_owner(down_term)],
        3,
    )
    gain_two_grad = jnp.sum(normed_two_grad * scaled_two, axis=0)
    residual_grad = own_cotangent.astype(f32) + norm_back(
        normed_two_grad, scaled_two, inverse_two, gain_two
    )
    residual_low = residual_grad.astype(low)
    mixed_grad = jnp.einsum("rw,gdw->grd", residual_low, w_out, preferred_element_type=f32)
    out_term = jnp.einsum("grd,rw->gdw", mixed, residual_low, preferred_element_type=f32)
    out_term = out_term.astype(low).reshape(width, width)
    head_grad, out_owned = exchange(
        ["swap", "reduce"], [mixed_grad.astype(low), by_owner(out_term)], 4
    )
    head_grad = whole(head_grad).reshape(seq_dev, length, local_heads, HEAD_DIM)
    head_grad = head_grad.transpose(0, 2, 1, 3)
    delta = jnp.sum(head_grad.astype(f32) * attended.astype(f32), axis=-1, keepdims=True)
    value_grad = jnp.einsum("bhqk,bhqd->bhkd", probs_low, head_grad, preferred_element_type=f32)
    prob_grad = jnp.einsum("bhqd,bhkd->bhqk", head_grad, value, preferred_element_type=f32)
    score_grad = (probs * (prob_grad - delta)).astype(low)
    query_grad = jnp.einsum("bhqk,bhkd->bhqd", score_grad, key, preferred_element_type=f32) * scale
    key_grad = jnp.einsum("bhqk,bhqd->bhkd", score_grad, query, preferred_element_type=f32) * scale
    qkv_grad = jnp.concatenate(
        [
            to_rows(rotate(query_grad.astype(low).astype(f32), cosine, -sine).astype(low)),
            to_rows(rotate(key_grad.astype(low).astype(f32), cosine, -sine).astype(low)),
            to_rows(value_grad.astype(low)),
        ],
        axis=1,
    )
    normed_one_grad_part = dot(qkv_grad, w_qkv, 1, 1)
    gain_one_grad = jnp.sum(normed_one_grad_part * scaled_full, axis=0)

    qkv_term = dot(normed_one, qkv_grad, 0, 0).astype(low)
    gain_terms = jnp.stack(
        [gain_one_grad.reshape(fsdp_n, shard), gain_two_grad.reshape(fsdp_n, shard)], axis=1
    )
    parts = exchange(
        ["fold", "fold", "gather", "gather", "gather", "grad", "grad"],
        [spans(normed_one_grad_part.astype(low)), spans(ffn_part)]
        + [in_owned, down_owned, out_owned, by_owner(qkv_term), gain_terms],
        5,
    )
    normed_one_grad = parts[0]
    _, scaled_one, inverse_one = layer_norm(inputs, gain_one)
    input_grad = (
        residual_grad + norm_back(normed_one_grad, scaled_one, inverse_one, gain_one)
    ).astype(low)
    block_out = (residual + parts[1]).astype(low)
    in_all, down_all, out_all, qkv_all, gain_all = parts[2:]

    def columns_of(stack, sections, section):
        return jnp.concatenate(
            [
                stack[g][:, j * section : (j + 1) * section]
                for j in range(sections)
                for g in range(groups)
            ],
            axis=1,
        ).astype(f32)

    qkv_out = columns_of(qkv_all, 3, group_width)
    in_out = columns_of(in_all, 2, ff_part)
    down_out = down_all.transpose(0, 2, 1).reshape(ff, shard).astype(f32)
    out_out = jnp.sum(out_all.astype(f32), axis=0)
    gain_out = jnp.sum(gain_all, axis=0)
    return (
        block_out.reshape(seq_dev, span_len, width),
        input_grad.reshape(seq_dev, span_len, width),
        qkv_out,
        out_out,
        in_out,
        down_out,
        gain_out[0],
        gain_out[1],
    )


def solution(mesh):
    in_specs = (
        P("fsdp", "seq", None),
        P("fsdp", "seq"),
        P("fsdp"),
        P("fsdp", None),
        P("fsdp", None),
        P("fsdp"),
        P("fsdp", None),
        P(None, "fsdp"),
        P("fsdp", "seq", None),
    )
    out_specs = (
        P("fsdp", "seq", None),
        P("fsdp", "seq", None),
        P("fsdp", None),
        P("fsdp", None),
        P("fsdp", None),
        P(None, "fsdp"),
        P("fsdp"),
        P("fsdp"),
    )
    return jax.shard_map(local, mesh=mesh, in_specs=in_specs, out_specs=out_specs, check_vma=False)
```
